32 devices in a mesh: group: 2 (over x), seq: 16 (over z, y, core).
Axes of the slice: x: 2, y: 2, z: 4, core: 2. Of those that a mesh axis runs over, the one named last changes fastest.
Arguments:
- tokens: bfloat16 [256, 8192], P('group', 'seq'), parts along dimension 0, may hold values from -1700 to 1700
- gain: bfloat16 [8192], P('seq'), may hold values from 0.099609375 to 1.8984375
- w_query: bfloat16 [8192, 8192], P('seq'), may hold values from -0.0625 to 0.0625
- w_key: bfloat16 [1024, 8192], P('seq'), may hold values from -0.375 to 0.375
- w_value: bfloat16 [1024, 8192], P('seq'), may hold values from -0.0625 to 0.0625
- w_out: bfloat16 [8192, 8192], P('seq'), may hold values from -0.09375 to 0.09375
- prefix_cache: bfloat16 [2, 8192, 1024], P(None, ('group', 'seq')), parts along dimension 1, may hold values from -2700 to 2700
Outputs:
- mixed: bfloat16 [256, 8192], P('group', 'seq'), parts along dimension 0
The draws below stay inside these ranges and needn't reach their ends.
There are 2 independent parts, one for each index of `group`. The reference program is written for one: setup_inputs(seed, part) draws one part's arguments, and reference() takes and returns one part's arrays. A program takes and returns all parts, laid end to end along the dimension named above; an argument that names none is the same for every part. Nothing has to cross between parts.
All inputs are finite; a program needn't handle non-finite values.
Results may differ from the reference program's by a relative error of at most 0.014.
The reference program's roundings to bfloat16 on the way (of `normed`, `query`, `key_own`, `value_own` and `attention`) count: a program that leaves them out, or rounds other values in their place, can miss the bound.
Values may be sent and summed in bfloat16 or wider, within the bound.
A program may use at most 64 MiB of HBM per device.

```python
import math
import jax
import jax.numpy as jnp
from jax import lax

D = 8192
H = 64
KV = 8
DH = 128
R = 128
PREFIX = 4096


def draw_tokens(key, part):
    key_rows, key_cols, key_base = jax.random.split(key, 3)
    row_top = 10.0
    ramp_top = 10.0
    base = jnp.clip(jax.random.normal(key_base, (R, D)), -4.0, 4.0)
    row_scale = jnp.exp(jax.random.uniform(key_rows, (R, 1), minval=0.0, maxval=jnp.log(row_top)))
    ramp = jnp.exp(jnp.log(ramp_top) * jnp.arange(D, dtype=jnp.float32) / D)
    col_scale = ramp * jnp.exp(jax.random.uniform(key_cols, (D,), minval=-0.7, maxval=0.7))
    return (base * row_scale * col_scale[None, :]).astype(jnp.bfloat16)


def draw_prefix_cache(key, part):
    key_keys, key_values = jax.random.split(key, 2)
    cached_keys = 3.0 * jnp.clip(jax.random.normal(key_keys, (PREFIX, KV * DH)), -5.0, 5.0)
    cached_values = jnp.clip(jax.random.normal(key_values, (PREFIX, KV * DH)), -5.0, 5.0)
    return jnp.stack([cached_keys, cached_values]).astype(jnp.bfloat16)


def spiked(values, key, source, target, shards_of, factor):
    owner, partner = [(jnp.arange(values.shape[dim]) // (values.shape[dim] // shards_of)).reshape([-1 if axis == dim else 1 for axis in range(values.ndim)]) for dim in (source, target)]
    chosen = jax.random.permutation(key, shards_of)[partner]
    strong = (owner == chosen) | (owner == (partner + shards_of // 2) % shards_of)
    return jnp.where(strong, factor * values, values)


def level_of(rng, extent, shards, smallest, largest):
    level, own = 1.0, jax.random.fold_in(rng, 6)
    for dim, shards_of in shards:
        draws = jnp.exp(jax.random.uniform(jax.random.fold_in(own, dim), (shards_of,), jnp.float32, smallest / len(shards), largest / len(shards)))
        level = level * jnp.repeat(draws, extent[dim] // shards_of).reshape([-1 if axis == dim else 1 for axis in range(len(extent))])
    return level


def centred(rng, extent, deviation, bound, pieces=(), kind=jnp.bfloat16):
    level = level_of(rng, extent, pieces, -0.22, 0.18) if pieces else 1.0
    result = jax.random.normal(rng, extent, jnp.float32) * deviation * level
    return jnp.minimum(jnp.maximum(result, -bound), bound).astype(kind)


def bell_draw_with(rng, shape, scale, bound, shards, heavy, kind=jnp.bfloat16):
    values = scale * jax.random.normal(rng, shape, jnp.float32)
    if shards:
        values = values * level_of(rng, shape, shards, -0.22, 0.18)
    return jnp.clip(spiked(values, jax.random.fold_in(rng, 3), *heavy), -bound, bound).astype(kind)


def setup_inputs(seed: int = 0, part: int = 0) -> dict:
    splits = jax.random.split(jax.random.key(seed), 8)
    own_keys = jax.random.split(jax.random.fold_in(splits[7], part), 8)
    return {
        "tokens": draw_tokens(jax.random.fold_in(jax.random.fold_in(splits[7], part), 71), part),
        "gain": jnp.clip(1.0 + 0.18 * jax.random.normal(splits[1], (D,), jnp.float32), 0.099609375, 1.8984375).astype(jnp.bfloat16),
        "w_query": centred(splits[2], (H * DH, D), D ** -0.5, 0.0625, ((0, 16),)),
        "w_key": centred(splits[3], (KV * DH, D), (D // 36) ** -0.5, 0.375, ((0, 16),)),
        "w_value": centred(splits[4], (KV * DH, D), D ** -0.5, 0.0625, ((0, 16),)),
        "w_out": bell_draw_with(splits[5], (H * DH, D), (H * DH) ** -0.5, 0.09375, ((0, 16),), (0, 1, 16, 2.0)),
        "prefix_cache": draw_prefix_cache(jax.random.fold_in(jax.random.fold_in(splits[7], part), 71), part),
    }


def normalize(tokens, gain):
    wide_tokens = tokens.astype(jnp.float32)
    inverse = lax.rsqrt(lax.optimization_barrier(jnp.mean(wide_tokens * wide_tokens, axis=1, keepdims=True)) + 1e-05)
    return (wide_tokens * inverse * gain.astype(jnp.float32)).astype(jnp.bfloat16)

def reference(tokens, gain, w_query, w_key, w_value, w_out, prefix_cache):
    contract_dims = (((1,), (1,)), ((), ()))
    normed = normalize(tokens, gain)
    query = lax.dot_general(normed, w_query, contract_dims, preferred_element_type=jnp.float32).astype(jnp.bfloat16)
    key_own = lax.dot_general(normed, w_key, contract_dims, preferred_element_type=jnp.float32).astype(jnp.bfloat16)
    value_own = lax.dot_general(normed, w_value, contract_dims, preferred_element_type=jnp.float32).astype(jnp.bfloat16)
    row_count = tokens.shape[0]
    group_size = H // KV
    score_scale = 1.0 / math.sqrt(DH)
    query_heads = query.reshape(row_count, KV, group_size, DH).astype(jnp.float32)
    key_heads = key_own.reshape(row_count, KV, DH).astype(jnp.float32)
    own_scores = jnp.einsum('rgjd,rgd->rgj', query_heads, key_heads) * score_scale
    value_heads = value_own.reshape(row_count, KV, DH)
    results = []
    for head_group in range(KV):
        query_group = query.reshape(row_count, KV, group_size * DH)[:, head_group].reshape(row_count * group_size, DH)
        keys_group = prefix_cache[0][:, head_group * DH:(head_group + 1) * DH]
        values_group = prefix_cache[1][:, head_group * DH:(head_group + 1) * DH]
        scores = lax.dot_general(query_group, keys_group, contract_dims, preferred_element_type=jnp.float32) * score_scale
        own_group = own_scores[:, head_group].reshape(row_count * group_size)
        row_max = jnp.maximum(lax.optimization_barrier(jnp.max(scores, axis=1)), own_group)
        weights = jnp.exp(scores - row_max[:, None])
        own_weight = jnp.exp(own_group - row_max)
        denominator = lax.optimization_barrier(jnp.sum(weights, axis=1)) + own_weight
        numerator = jnp.dot(weights.astype(jnp.bfloat16), values_group, preferred_element_type=jnp.float32)
        own_values = jnp.repeat(value_heads[:, head_group], group_size, axis=0).astype(jnp.float32)
        rounded = lax.optimization_barrier(own_weight.astype(jnp.bfloat16)).astype(jnp.float32)
        numerator = numerator + rounded[:, None] * own_values
        results.append((numerator / denominator[:, None]).astype(jnp.bfloat16).reshape(row_count, group_size * DH))
    attention = jnp.concatenate(results, axis=1)
    return jnp.dot(attention, w_out, preferred_element_type=jnp.float32).astype(jnp.bfloat16)
```

```python
import functools
import math

import jax
import jax.numpy as jnp
from jax import lax
from jax.experimental import pallas as pl
from jax.experimental.pallas import tpu as pltpu
from jax.sharding import PartitionSpec as P

H = 64
KV = 8
DH = 128
CHUNKS = 2
NT = (((1,), (1,)), ((), ()))
MESH = pl.DeviceIdType.MESH
F32 = jnp.float32
BF16 = jnp.bfloat16


def kernel(
    n, ny, tokens, gain_in, w_query, w_key, w_value, w_out, cache, out,
    tok, my_gain, gains, normed, wq, wk, wv, wo, q_acc, k_acc, v_acc, q_rows, k_own, v_own,
    k_buf, v_buf, scores, top, low, numer, att, acc, s1_out, s1_in, s2_out, s2_in, s3_out, s3_in,
    local_sem, gain_send, gain_recv, tok_up, tok_down, tok_send_y, tok_send_c, tok_recv,
    k_send, k_send_c, k_recv, v_send, v_send_c, v_recv, own_send, own_recv,
    s1_send, s1_recv, s2_send, s2_recv, s3_send, s3_recv,
):
    chips = n // 2
    nz = chips // ny
    me = lax.axis_index("seq")
    c = lax.rem(me, 2)
    chip = me // 2
    y = lax.rem(chip, ny)
    z = chip // ny
    partner = chip * 2 + 1 - c
    rows, width = tokens.shape
    heads = H // n
    members = n // KV
    kv_head = me // members
    member = lax.rem(me, members)
    positions = cache.shape[1]
    lanes = [slice(k * 128, (k + 1) * 128) for k in range(positions // 128)]
    scale = 1.0 / math.sqrt(DH)

    def seq_of(z_, y_, c_):
        return (z_ * ny + y_) * 2 + c_

    def other_z(d):
        return lax.rem(z + d, nz)

    def other_y(d):
        return lax.rem(y + d, ny)

    def remote(src, dst, send, recv, to):
        return pltpu.make_async_remote_copy(
            src_ref=src, dst_ref=dst, send_sem=send, recv_sem=recv,
            device_id={"seq": to}, device_id_type=MESH,
        )

    def each(start, stop, step):
        lax.fori_loop(start, stop, lambda i, carry: (step(i), carry)[1], 0)

    weights_in = [
        pltpu.make_async_copy(src, dst, local_sem.at[i])
        for i, (src, dst) in enumerate(
            [(w_query, wq), (w_key, wk), (w_value, wv), (w_out, wo)]
        )
    ]
    own_tok = pltpu.make_async_copy(tokens, tok.at[me], local_sem.at[4])
    gain = my_gain
    my_gain[...] = gain_in[...].astype(F32).reshape(1, width)
    gains[me] = my_gain[...]

    def own_cols(to_kv):
        return pl.ds(pl.multiple_of(to_kv * DH, DH), DH)

    own_k = pltpu.make_async_copy(
        cache.at[0, :, own_cols(kv_head)], k_buf.at[me], local_sem.at[6]
    )
    own_v = pltpu.make_async_copy(
        cache.at[1, :, own_cols(kv_head)], v_buf.at[me], local_sem.at[7]
    )
    for copy in weights_in:
        copy.start()
    own_tok.start()

    barrier = pltpu.get_barrier_semaphore()
    each(1, n, lambda i: pl.semaphore_signal(
        barrier, inc=1, device_id={"seq": lax.rem(me + i, n)}, device_id_type=MESH))
    pl.semaphore_wait(barrier, n - 1)

    chunks = tok_recv.shape[1]
    deep = rows // chunks

    def piece_of(slot, k):
        return tok.at[slot, pl.ds(pl.multiple_of(k * deep, deep), deep), :]

    def tok_z(slot, k, d, up):
        ends = tok_up if up else tok_down
        to = jnp.clip(z + (1 if up else -1), 0, nz - 1)
        return remote(piece_of(slot, k), piece_of(slot, k), ends.at[d, k],
                      tok_recv.at[slot, k], seq_of(to, y, c))

    def tok_y(slot, k, d_z, d_y):
        return remote(piece_of(slot, k), piece_of(slot, k), tok_send_y.at[d_z, d_y, k],
                      tok_recv.at[slot, k], seq_of(z, other_y(d_y), c))

    def tok_c(slot, k):
        return remote(piece_of(slot, k), piece_of(slot, k), tok_send_c.at[slot // 2, k],
                      tok_recv.at[slot, k], partner)

    def tok_wait(slot, k):
        remote(piece_of(slot, k), piece_of(slot, k), tok_send_c.at[0, k], tok_recv.at[slot, k],
               partner).wait_recv()

    own_tok.wait()

    def send_own(k):
        @pl.when(z + 1 < nz)
        def _():
            tok_z(me, k, 0, True).start()

        @pl.when(z >= 1)
        def _():
            tok_z(me, k, 0, False).start()

        for d_y in range(1, ny):
            tok_y(me, k, z, d_y).start()
        tok_c(me, k).start()

    each(0, chunks, send_own)

    def gain_copy(i):
        return remote(gain, gains.at[me], gain_send.at[i], gain_recv.at[me], lax.rem(me + i, n))

    each(1, n, lambda i: gain_copy(i).start())

    def kv_copy(half, buf, send, recv, i):
        other = lax.rem(chip + i, chips)
        to = other * 2 + c
        return remote(cache.at[half, :, own_cols(to // members)], buf.at[me], send.at[i],
                      recv.at[me], to)

    def kv_pair(src, buf, send, recv, slot):
        return remote(src, buf.at[slot], send.at[slot // 2], recv.at[slot], partner)

    def kv_wait(buf, send, recv, slot):
        remote(buf.at[slot], buf.at[slot], send.at[0], recv.at[slot], partner).wait_recv()

    def k_copy(i):
        return kv_copy(0, k_buf, k_send, k_recv, i)

    def v_copy(i):
        return kv_copy(1, v_buf, v_send, v_recv, i)


    def forward_z(i):
        d = 1 + i // chunks
        k = lax.rem(i, chunks)

        def pass_on(slot, up):
            tok_wait(slot, k)

            @pl.when((z + 1 < nz) if up else (z >= 1))
            def _():
                tok_z(slot, k, d, up).start()

            for d_y in range(1, ny):
                tok_y(slot, k, slot // (2 * ny), d_y).start()
            tok_c(slot, k).start()

        @pl.when(z - d >= 0)
        def _():
            pass_on(seq_of(z - d, y, c), True)

        @pl.when(z + d < nz)
        def _():
            pass_on(seq_of(z + d, y, c), False)

    each(0, (nz - 1) * chunks, forward_z)
    each(1, chips, lambda i: k_copy(i).start())
    k_own_src = cache.at[0, :, own_cols(kv_head)]
    v_own_src = cache.at[1, :, own_cols(kv_head)]
    kv_pair(k_own_src, k_buf, k_send_c, k_recv, me).start()
    own_k.start()


    def spread(i):
        reach = jnp.minimum(z, nz - 1 - z)
        side = jnp.where(lax.rem(i, 2) == 1, z - (i + 1) // 2, z + i // 2)
        return jnp.where(i <= 2 * reach, side, jnp.where(z < nz - 1 - z, i, nz - 1 - i))

    for d_y in range(1, ny):
        def forward_y(i, d_y=d_y):
            there = seq_of(spread(i // chunks), other_y(d_y), c)
            k = lax.rem(i, chunks)
            tok_wait(there, k)
            tok_c(there, k).start()
        each(0, nz * chunks, forward_y)

    each(1, chips, lambda i: v_copy(i).start())
    kv_pair(v_own_src, v_buf, v_send_c, v_recv, me).start()
    own_v.start()

    each(0, chips * chunks, lambda i: tok_wait((i // chunks) * 2 + 1 - c, lax.rem(i, chunks)))

    def gain_wait(i):
        slot = lax.rem(me + i, n)
        remote(gain, gains.at[slot], gain_send.at[0], gain_recv.at[slot], partner).wait_recv()

    each(1, n, gain_wait)

    parts = width // 128

    def square_step(b, total):
        x = tok[b].astype(F32)
        for k in range(parts):
            piece = x[:, k * 128:(k + 1) * 128]
            total = total + piece * piece
        return total

    total = lax.fori_loop(0, n, square_step, jnp.zeros((rows, 128), F32))
    mean = jnp.sum(total, axis=1, keepdims=True) * (1.0 / (n * width))
    inverse = jnp.broadcast_to(lax.rsqrt(mean + 1e-05), (rows, 128))

    def norm_step(b):
        for k in range(parts):
            x = tok[b, :, k * 128:(k + 1) * 128].astype(F32)
            g = gains[b, :, k * 128:(k + 1) * 128].astype(F32)
            normed[:, pl.ds(pl.multiple_of(b * width + k * 128, 128), 128)] = (
                x * inverse * g).astype(BF16)

    each(0, n, norm_step)

    for copy in weights_in[:3]:
        copy.wait()
    q_acc[...] = jnp.zeros_like(q_acc)
    k_acc[...] = jnp.zeros_like(k_acc)
    v_acc[...] = jnp.zeros_like(v_acc)
    depth = 1024

    def project(i):
        cols = pl.ds(pl.multiple_of(i * depth, depth), depth)
        x = normed[:, cols]
        k_acc[...] += lax.dot_general(wk[:, cols], x, NT, preferred_element_type=F32)
        v_acc[...] += lax.dot_general(wv[:, cols], x, NT, preferred_element_type=F32)
        q_acc[...] += lax.dot_general(x, wq[:, cols], NT, preferred_element_type=F32)

    each(0, normed.shape[1] // depth, project)
    k_own[member] = k_acc[...].astype(BF16)
    v_own[member] = v_acc[...].astype(BF16)

    def own_copy(which, buf, i):
        return remote(buf.at[member], buf.at[member], own_send.at[which, i],
                      own_recv.at[which, member], kv_head * members + lax.rem(member + i, members))

    def own_wait(which, buf, i):
        slot = lax.rem(member + i, members)
        remote(buf.at[slot], buf.at[slot], own_send.at[which, 0], own_recv.at[which, slot],
               partner).wait_recv()

    for i in range(1, members):
        own_copy(0, k_own, i).start()
        own_copy(1, v_own, i).start()

    for h in range(heads):
        q_rows[h * rows:(h + 1) * rows, :] = q_acc[:, h * DH:(h + 1) * DH].astype(BF16)

    top[...] = jnp.full_like(top, -jnp.inf)

    def score_block(slot):
        keys = k_buf[slot]
        for h in range(heads):
            here = slice(h * rows, (h + 1) * rows)
            s = lax.dot_general(q_rows[here, :], keys, NT, preferred_element_type=F32) * scale
            scores[slot, here, :] = s
            best = top[here, :]
            for part in lanes:
                best = jnp.maximum(best, s[:, part])
            top[here, :] = best

    own_k.wait()
    score_block(me)

    def k_mine(i):
        slot = lax.rem(chip + chips - i, chips) * 2 + c
        kv_wait(k_buf, k_send_c, k_recv, slot)
        kv_pair(k_buf.at[slot], k_buf, k_send_c, k_recv, slot).start()
        score_block(slot)

    each(1, chips, k_mine)

    def k_theirs(i):
        slot = lax.rem(chip + chips - i, chips) * 2 + 1 - c
        kv_wait(k_buf, k_send_c, k_recv, slot)
        score_block(slot)

    each(0, chips, k_theirs)

    for i in range(1, members):
        own_wait(0, k_own, i)
        own_wait(1, v_own, i)
    key_rows = k_own[...].astype(F32).reshape(DH, rows).T
    own_scores = []
    for h in range(heads):
        here = slice(h * rows, (h + 1) * rows)
        own = jnp.sum(q_rows[here, :].astype(F32) * key_rows, axis=1, keepdims=True) * scale
        best = jnp.maximum(jnp.max(top[here, :], axis=1, keepdims=True), own)
        top[here, :] = jnp.broadcast_to(best, (rows, 128))
        own_scores.append(jnp.exp(own - best))

    low[...] = jnp.zeros_like(low)
    numer[...] = jnp.zeros_like(numer)

    def value_block(slot):
        values = v_buf[slot]
        for h in range(heads):
            here = slice(h * rows, (h + 1) * rows)
            best = top[here, :]
            pieces = [jnp.exp(scores[slot, here, part] - best) for part in lanes]
            low[here, :] += functools.reduce(jnp.add, pieces)
            weights = jnp.concatenate([piece.astype(BF16) for piece in pieces], axis=1)
            numer[here, :] += jnp.dot(weights, values, preferred_element_type=F32)

    own_v.wait()
    value_block(me)

    def v_mine(i):
        slot = lax.rem(chip + chips - i, chips) * 2 + c
        kv_wait(v_buf, v_send_c, v_recv, slot)
        kv_pair(v_buf.at[slot], v_buf, v_send_c, v_recv, slot).start()
        value_block(slot)

    each(1, chips, v_mine)

    def v_theirs(i):
        slot = lax.rem(chip + chips - i, chips) * 2 + 1 - c
        kv_wait(v_buf, v_send_c, v_recv, slot)
        value_block(slot)

    each(0, chips, v_theirs)

    value_rows = v_own[...].astype(F32).reshape(DH, rows).T
    for h in range(heads):
        here = slice(h * rows, (h + 1) * rows)
        own_weight = own_scores[h]
        denom = jnp.sum(low[here, :], axis=1, keepdims=True) + own_weight
        total = numer[here, :] + own_weight.astype(BF16).astype(F32) * value_rows
        att[:, h * DH:(h + 1) * DH] = (total / denom).astype(BF16)

    weights_in[3].wait()

    def partial_for(to):
        cols = pl.ds(pl.multiple_of(to * width, width), width)
        return jnp.dot(att[...], wo[:, cols], preferred_element_type=F32)

    def s1_copy(target):
        return remote(s1_out.at[target], s1_in.at[target], s1_send.at[target],
                      s1_recv.at[target], partner)

    def s2_copy(d_z, d_y):
        return remote(s2_out.at[d_z, d_y], s2_in.at[d_z, d_y], s2_send.at[d_z, d_y],
                      s2_recv.at[d_z, d_y], seq_of(z, other_y(d_y), c))

    def s3_copy(d):
        return remote(s3_out.at[d], s3_in.at[d], s3_send.at[d], s3_recv.at[d],
                      seq_of(other_z(d), y, c))

    def chip_sum(target):
        s1_copy(target).wait_recv()
        return acc[target] + s1_in[target].astype(F32)

    def distance(i):
        half = nz // 2
        middle = jnp.where(i < half, i, i + 1)
        return jnp.where(i == 0, half % nz, jnp.where(i == nz - 1, 0, middle))

    def give(i, d_y):
        target = other_z(distance(i)) * ny + other_y(d_y)
        s1_out[target] = partial_for(target * 2 + 1 - c).astype(BF16)
        s1_copy(target).start()

    def keep(i, d_y):
        target = other_z(distance(i)) * ny + other_y(d_y)
        acc[target] = partial_for(target * 2 + c)

    def step_two(i, d_y):
        d = distance(i)
        keep(i, d_y)
        s2_out[d, d_y] = chip_sum(other_z(d) * ny + other_y(d_y)).astype(BF16)
        s2_copy(d, d_y).start()

    def column_sum(d):
        total = chip_sum(other_z(d) * ny + y)
        for d_y in range(1, ny):
            s2_copy(d, d_y).wait_recv()
            total = total + s2_in[d, d_y].astype(F32)
        return total

    def step_three(i):
        d = distance(i)
        s3_out[d] = column_sum(d).astype(BF16)
        s3_copy(d).start()

    for d_y in range(1, ny):
        each(0, nz, functools.partial(give, d_y=d_y))
    for d_y in range(1, ny):
        each(0, nz, functools.partial(step_two, d_y=d_y))
    each(0, nz, functools.partial(give, d_y=0))
    each(0, nz, functools.partial(keep, d_y=0))
    each(0, nz - 1, step_three)
    acc[chip] = column_sum(0)

    def last(d):
        s3_copy(d).wait_recv()
        acc[chip] += s3_in[d].astype(F32)

    each(1, nz, last)
    out[...] = acc[chip].astype(out.dtype)

    def tok_sent(i):
        d = i // chunks
        k = lax.rem(i, chunks)

        @pl.when((z - d >= 0) & (z + 1 < nz))
        def _():
            tok_z(seq_of(z - d, y, c), k, d, True).wait_send()

        @pl.when((z + d < nz) & (z >= 1))
        def _():
            tok_z(seq_of(z + d, y, c), k, d, False).wait_send()

        for d_y in range(1, ny):
            tok_y(me, k, d, d_y).wait_send()

    each(0, nz * chunks, tok_sent)
    each(0, chips * chunks, lambda i: tok_c(
        (i // chunks) * 2 + c, lax.rem(i, chunks)).wait_send())
    each(1, n, lambda i: gain_copy(i).wait_send())
    each(1, chips, lambda i: k_copy(i).wait_send())
    each(1, chips, lambda i: v_copy(i).wait_send())

    def core_sent(i):
        slot = i * 2 + c
        kv_pair(k_buf.at[slot], k_buf, k_send_c, k_recv, slot).wait_send()
        kv_pair(v_buf.at[slot], v_buf, v_send_c, v_recv, slot).wait_send()
        s1_copy(i).wait_send()

    each(0, chips, core_sent)
    for i in range(1, members):
        own_copy(0, k_own, i).wait_send()
        own_copy(1, v_own, i).wait_send()
    for d_y in range(1, ny):
        each(0, nz, lambda d, d_y=d_y: s2_copy(d, d_y).wait_send())
    each(1, nz, lambda d: s3_copy(d).wait_send())


def body(n, ny, tokens, gain, w_query, w_key, w_value, w_out, cache):
    rows, width = tokens.shape
    features = w_query.shape[1]
    heads = H // n
    chips = n // 2
    nz = chips // ny
    members = n // KV
    own = w_key.shape[0]
    positions = cache.shape[1]
    stack = heads * rows
    dma = pltpu.SemaphoreType.DMA
    hbm = pl.BlockSpec(memory_space=pl.ANY)
    vmem = pl.BlockSpec(memory_space=pltpu.VMEM)
    block = (rows, width)
    return pl.pallas_call(
        functools.partial(kernel, n, ny),
        out_shape=jax.ShapeDtypeStruct((rows, width), BF16),
        in_specs=[vmem, vmem, hbm, hbm, hbm, hbm, hbm],
        out_specs=vmem,
        scratch_shapes=[
            pltpu.VMEM((n, rows, width), BF16),
            pltpu.VMEM((1, width), F32),
            pltpu.VMEM((n, 1, width), F32),
            pltpu.VMEM((rows, features), BF16),
            pltpu.VMEM(w_query.shape, BF16),
            pltpu.VMEM(w_key.shape, BF16),
            pltpu.VMEM(w_value.shape, BF16),
            pltpu.VMEM(w_out.shape, BF16),
            pltpu.VMEM((rows, heads * DH), F32),
            pltpu.VMEM((own, rows), F32),
            pltpu.VMEM((own, rows), F32),
            pltpu.VMEM((stack, DH), BF16),
            pltpu.VMEM((members, own, rows), BF16),
            pltpu.VMEM((members, own, rows), BF16),
            pltpu.VMEM((n, positions, DH), BF16),
            pltpu.VMEM((n, positions, DH), BF16),
            pltpu.VMEM((n, stack, positions), F32),
            pltpu.VMEM((stack, 128), F32),
            pltpu.VMEM((stack, 128), F32),
            pltpu.VMEM((stack, DH), F32),
            pltpu.VMEM((rows, heads * DH), BF16),
            pltpu.VMEM((chips,) + block, F32),
            pltpu.VMEM((chips,) + block, BF16),
            pltpu.VMEM((chips,) + block, BF16),
            pltpu.VMEM((nz, ny) + block, BF16),
            pltpu.VMEM((nz, ny) + block, BF16),
            pltpu.VMEM((nz,) + block, BF16),
            pltpu.VMEM((nz,) + block, BF16),
            dma((8,)),
            dma((n,)), dma((n,)),
            dma((nz, CHUNKS)), dma((nz, CHUNKS)), dma((nz, ny, CHUNKS)), dma((chips, CHUNKS)),
            dma((n, CHUNKS)),
            dma((chips,)), dma((chips,)), dma((n,)),
            dma((chips,)), dma((chips,)), dma((n,)),
            dma((2, members)), dma((2, members)),
            dma((chips,)), dma((chips,)),
            dma((nz, ny)), dma((nz, ny)),
            dma((nz,)), dma((nz,)),
        ],
        compiler_params=pltpu.CompilerParams(
            collective_id=0, has_side_effects=True, vmem_limit_bytes=60 * 2**20
        ),
    )(tokens, gain, w_query, w_key, w_value, w_out, cache)


def solution(mesh):
    n = mesh.shape["seq"]
    ny = max(1, 4 // mesh.shape["group"])
    return jax.shard_map(
        functools.partial(body, n, ny),
        mesh=mesh,
        in_specs=(
            P("group", "seq"),
            P("seq"),
            P("seq", None),
            P("seq", None),
            P("seq", None),
            P("seq", None),
            P(None, ("group", "seq"), None),
        ),
        out_specs=P("group", "seq"),
        check_vma=False,
    )
```

```python
import functools
import math

import jax
import jax.numpy as jnp
from jax import lax
from jax.experimental import pallas as pl
from jax.experimental.pallas import tpu as pltpu
from jax.sharding import PartitionSpec as P

H = 64
KV = 8
DH = 128
CHUNKS = 2
NT = (((1,), (1,)), ((), ()))
MESH = pl.DeviceIdType.MESH
F32 = jnp.float32
BF16 = jnp.bfloat16


def kernel(
    n, ny, tokens, gain_in, w_query, w_key, w_value, w_out, cache, out,
    tok, my_gain, gains, normed, wq, wk, wv, wo, q_acc, k_acc, v_acc, q_rows, k_own, v_own,
    k_buf, v_buf, scores, top, low, numer, att, acc, s1_out, s1_in, s2_out, s2_in, s3_out, s3_in,
    local_sem, gain_send, gain_recv, tok_up, tok_down, tok_send_y, tok_send_c, tok_recv,
    k_send, k_send_c, k_recv, v_send, v_send_c, v_recv, own_send, own_recv,
    s1_send, s1_recv, s2_send, s2_recv, s3_send, s3_recv,
):
    chips = n // 2
    nz = chips // ny
    me = lax.axis_index("seq")
    c = lax.rem(me, 2)
    chip = me // 2
    y = lax.rem(chip, ny)
    z = chip // ny
    partner = chip * 2 + 1 - c
    rows, width = tokens.shape
    heads = H // n
    members = n // KV
    kv_head = me // members
    member = lax.rem(me, members)
    positions = cache.shape[1]
    lanes = [slice(k * 128, (k + 1) * 128) for k in range(positions // 128)]
    scale = 1.0 / math.sqrt(DH)

    def seq_of(z_, y_, c_):
        return (z_ * ny + y_) * 2 + c_

    def other_z(d):
        return lax.rem(z + d, nz)

    def other_y(d):
        return lax.rem(y + d, ny)

    def remote(src, dst, send, recv, to):
        return pltpu.make_async_remote_copy(
            src_ref=src, dst_ref=dst, send_sem=send, recv_sem=recv,
            device_id={"seq": to}, device_id_type=MESH,
        )

    def each(start, stop, step):
        lax.fori_loop(start, stop, lambda i, carry: (step(i), carry)[1], 0)

    weights_in = [
        pltpu.make_async_copy(src, dst, local_sem.at[i])
        for i, (src, dst) in enumerate(
            [(w_query, wq), (w_key, wk), (w_value, wv), (w_out, wo)]
        )
    ]
    own_tok = pltpu.make_async_copy(tokens, tok.at[me], local_sem.at[4])
    gain = my_gain
    my_gain[...] = gain_in[...].astype(F32).reshape(1, width)
    gains[me] = my_gain[...]

    def own_cols(to_kv):
        return pl.ds(pl.multiple_of(to_kv * DH, DH), DH)

    own_k = pltpu.make_async_copy(
        cache.at[0, :, own_cols(kv_head)], k_buf.at[me], local_sem.at[6]
    )
    own_v = pltpu.make_async_copy(
        cache.at[1, :, own_cols(kv_head)], v_buf.at[me], local_sem.at[7]
    )
    for copy in weights_in:
        copy.start()
    own_tok.start()

    barrier = pltpu.get_barrier_semaphore()

    def greet(to):
        pl.semaphore_signal(barrier, inc=1, device_id={"seq": to}, device_id_type=MESH)

    @pl.when(z >= 1)
    def _():
        greet(seq_of(z - 1, y, c))

    @pl.when(z + 1 < nz)
    def _():
        greet(seq_of(z + 1, y, c))

    for d_y in range(1, ny):
        greet(seq_of(z, other_y(d_y), c))
        greet(seq_of(z, other_y(d_y), 1 - c))
    greet(partner)
    pl.semaphore_wait(
        barrier, 2 * ny - 1 + jnp.where(z >= 1, 1, 0) + jnp.where(z + 1 < nz, 1, 0))

    chunks = tok_recv.shape[1]
    deep = rows // chunks

    def piece_of(slot, k):
        return tok.at[slot, pl.ds(pl.multiple_of(k * deep, deep), deep), :]

    def tok_z(slot, k, d, up):
        ends = tok_up if up else tok_down
        to = jnp.clip(z + (1 if up else -1), 0, nz - 1)
        return remote(piece_of(slot, k), piece_of(slot, k), ends.at[d, k],
                      tok_recv.at[slot, k], seq_of(to, y, c))

    def tok_y(slot, k, d_z, d_y):
        return remote(piece_of(slot, k), piece_of(slot, k), tok_send_y.at[d_z, d_y, k],
                      tok_recv.at[slot, k], seq_of(z, other_y(d_y), c))

    def tok_c(slot, k):
        return remote(piece_of(slot, k), piece_of(slot, k), tok_send_c.at[slot // 2, k],
                      tok_recv.at[slot, k], partner)

    def tok_wait(slot, k):
        remote(piece_of(slot, k), piece_of(slot, k), tok_send_c.at[0, k], tok_recv.at[slot, k],
               partner).wait_recv()

    own_tok.wait()

    def send_own(k):
        @pl.when(z + 1 < nz)
        def _():
            tok_z(me, k, 0, True).start()

        @pl.when(z >= 1)
        def _():
            tok_z(me, k, 0, False).start()

        for d_y in range(1, ny):
            tok_y(me, k, z, d_y).start()
        tok_c(me, k).start()

    each(0, chunks, send_own)

    def gain_copy(i):
        return remote(gain, gains.at[me], gain_send.at[i], gain_recv.at[me], lax.rem(me + i, n))


    def kv_copy(half, buf, send, recv, i):
        other = lax.rem(chip + i, chips)
        to = other * 2 + c
        return remote(cache.at[half, :, own_cols(to // members)], buf.at[me], send.at[i],
                      recv.at[me], to)

    def kv_pair(src, buf, send, recv, slot):
        return remote(src, buf.at[slot], send.at[slot // 2], recv.at[slot], partner)

    def kv_wait(buf, send, recv, slot):
        remote(buf.at[slot], buf.at[slot], send.at[0], recv.at[slot], partner).wait_recv()

    def k_copy(i):
        return kv_copy(0, k_buf, k_send, k_recv, i)

    def v_copy(i):
        return kv_copy(1, v_buf, v_send, v_recv, i)


    def forward_z(i):
        d = 1 + i // chunks
        k = lax.rem(i, chunks)

        def pass_on(slot, up):
            tok_wait(slot, k)

            @pl.when((z + 1 < nz) if up else (z >= 1))
            def _():
                tok_z(slot, k, d, up).start()

            for d_y in range(1, ny):
                tok_y(slot, k, slot // (2 * ny), d_y).start()
            tok_c(slot, k).start()

        @pl.when(z - d >= 0)
        def _():
            pass_on(seq_of(z - d, y, c), True)

        @pl.when(z + d < nz)
        def _():
            pass_on(seq_of(z + d, y, c), False)

    each(0, (nz - 1) * chunks, forward_z)
    each(1, n, lambda i: gain_copy(i).start())
    each(1, chips, lambda i: k_copy(i).start())
    k_own_src = cache.at[0, :, own_cols(kv_head)]
    v_own_src = cache.at[1, :, own_cols(kv_head)]
    kv_pair(k_own_src, k_buf, k_send_c, k_recv, me).start()
    own_k.start()


    def spread(i):
        reach = jnp.minimum(z, nz - 1 - z)
        side = jnp.where(lax.rem(i, 2) == 1, z - (i + 1) // 2, z + i // 2)
        return jnp.where(i <= 2 * reach, side, jnp.where(z < nz - 1 - z, i, nz - 1 - i))

    for d_y in range(1, ny):
        def forward_y(i, d_y=d_y):
            there = seq_of(spread(i // chunks), other_y(d_y), c)
            k = lax.rem(i, chunks)
            tok_wait(there, k)
            tok_c(there, k).start()
        each(0, nz * chunks, forward_y)

    each(1, chips, lambda i: v_copy(i).start())
    kv_pair(v_own_src, v_buf, v_send_c, v_recv, me).start()
    own_v.start()

    each(0, chips * chunks, lambda i: tok_wait((i // chunks) * 2 + 1 - c, lax.rem(i, chunks)))

    def gain_wait(i):
        slot = lax.rem(me + i, n)
        remote(gain, gains.at[slot], gain_send.at[0], gain_recv.at[slot], partner).wait_recv()

    each(1, n, gain_wait)

    parts = width // 128

    def square_step(b, total):
        x = tok[b].astype(F32)
        for k in range(parts):
            piece = x[:, k * 128:(k + 1) * 128]
            total = total + piece * piece
        return total

    total = lax.fori_loop(0, n, square_step, jnp.zeros((rows, 128), F32))
    mean = jnp.sum(total, axis=1, keepdims=True) * (1.0 / (n * width))
    inverse = jnp.broadcast_to(lax.rsqrt(mean + 1e-05), (rows, 128))

    def norm_step(b):
        for k in range(parts):
            x = tok[b, :, k * 128:(k + 1) * 128].astype(F32)
            g = gains[b, :, k * 128:(k + 1) * 128].astype(F32)
            normed[:, pl.ds(pl.multiple_of(b * width + k * 128, 128), 128)] = (
                x * inverse * g).astype(BF16)

    each(0, n, norm_step)

    for copy in weights_in[:3]:
        copy.wait()
    q_acc[...] = jnp.zeros_like(q_acc)
    k_acc[...] = jnp.zeros_like(k_acc)
    v_acc[...] = jnp.zeros_like(v_acc)
    depth = 1024

    def project(i):
        cols = pl.ds(pl.multiple_of(i * depth, depth), depth)
        x = normed[:, cols]
        k_acc[...] += lax.dot_general(wk[:, cols], x, NT, preferred_element_type=F32)
        v_acc[...] += lax.dot_general(wv[:, cols], x, NT, preferred_element_type=F32)
        q_acc[...] += lax.dot_general(x, wq[:, cols], NT, preferred_element_type=F32)

    each(0, normed.shape[1] // depth, project)
    k_own[member] = k_acc[...].astype(BF16)
    v_own[member] = v_acc[...].astype(BF16)

    def own_copy(which, buf, i):
        return remote(buf.at[member], buf.at[member], own_send.at[which, i],
                      own_recv.at[which, member], kv_head * members + lax.rem(member + i, members))

    def own_wait(which, buf, i):
        slot = lax.rem(member + i, members)
        remote(buf.at[slot], buf.at[slot], own_send.at[which, 0], own_recv.at[which, slot],
               partner).wait_recv()

    for i in range(1, members):
        own_copy(0, k_own, i).start()
        own_copy(1, v_own, i).start()

    for h in range(heads):
        q_rows[h * rows:(h + 1) * rows, :] = q_acc[:, h * DH:(h + 1) * DH].astype(BF16)

    top[...] = jnp.full_like(top, -jnp.inf)

    def score_block(slot):
        keys = k_buf[slot]
        for h in range(heads):
            here = slice(h * rows, (h + 1) * rows)
            s = lax.dot_general(q_rows[here, :], keys, NT, preferred_element_type=F32) * scale
            scores[slot, here, :] = s
            best = top[here, :]
            for part in lanes:
                best = jnp.maximum(best, s[:, part])
            top[here, :] = best

    own_k.wait()
    score_block(me)

    def k_mine(i):
        slot = lax.rem(chip + chips - i, chips) * 2 + c
        kv_wait(k_buf, k_send_c, k_recv, slot)
        kv_pair(k_buf.at[slot], k_buf, k_send_c, k_recv, slot).start()
        score_block(slot)

    each(1, chips, k_mine)

    def k_theirs(i):
        slot = lax.rem(chip + chips - i, chips) * 2 + 1 - c
        kv_wait(k_buf, k_send_c, k_recv, slot)
        score_block(slot)

    each(0, chips, k_theirs)

    for i in range(1, members):
        own_wait(0, k_own, i)
        own_wait(1, v_own, i)
    key_rows = k_own[...].astype(F32).reshape(DH, rows).T
    own_scores = []
    for h in range(heads):
        here = slice(h * rows, (h + 1) * rows)
        own = jnp.sum(q_rows[here, :].astype(F32) * key_rows, axis=1, keepdims=True) * scale
        best = jnp.maximum(jnp.max(top[here, :], axis=1, keepdims=True), own)
        top[here, :] = jnp.broadcast_to(best, (rows, 128))
        own_scores.append(jnp.exp(own - best))

    low[...] = jnp.zeros_like(low)
    numer[...] = jnp.zeros_like(numer)

    def value_block(slot):
        values = v_buf[slot]
        for h in range(heads):
            here = slice(h * rows, (h + 1) * rows)
            best = top[here, :]
            pieces = [jnp.exp(scores[slot, here, part] - best) for part in lanes]
            low[here, :] += functools.reduce(jnp.add, pieces)
            weights = jnp.concatenate([piece.astype(BF16) for piece in pieces], axis=1)
            numer[here, :] += jnp.dot(weights, values, preferred_element_type=F32)

    own_v.wait()
    value_block(me)

    def v_mine(i):
        slot = lax.rem(chip + chips - i, chips) * 2 + c
        kv_wait(v_buf, v_send_c, v_recv, slot)
        kv_pair(v_buf.at[slot], v_buf, v_send_c, v_recv, slot).start()
        value_block(slot)

    each(1, chips, v_mine)

    def v_theirs(i):
        slot = lax.rem(chip + chips - i, chips) * 2 + 1 - c
        kv_wait(v_buf, v_send_c, v_recv, slot)
        value_block(slot)

    each(0, chips, v_theirs)

    value_rows = v_own[...].astype(F32).reshape(DH, rows).T
    for h in range(heads):
        here = slice(h * rows, (h + 1) * rows)
        own_weight = own_scores[h]
        denom = jnp.sum(low[here, :], axis=1, keepdims=True) + own_weight
        total = numer[here, :] + own_weight.astype(BF16).astype(F32) * value_rows
        att[:, h * DH:(h + 1) * DH] = (total / denom).astype(BF16)

    weights_in[3].wait()

    def partial_for(to):
        cols = pl.ds(pl.multiple_of(to * width, width), width)
        return jnp.dot(att[...], wo[:, cols], preferred_element_type=F32)

    def s1_copy(target):
        return remote(s1_out.at[target], s1_in.at[target], s1_send.at[target],
                      s1_recv.at[target], partner)

    def s2_copy(d_z, d_y):
        return remote(s2_out.at[d_z, d_y], s2_in.at[d_z, d_y], s2_send.at[d_z, d_y],
                      s2_recv.at[d_z, d_y], seq_of(z, other_y(d_y), c))

    def s3_copy(d):
        return remote(s3_out.at[d], s3_in.at[d], s3_send.at[d], s3_recv.at[d],
                      seq_of(other_z(d), y, c))

    def chip_sum(target):
        s1_copy(target).wait_recv()
        return acc[target] + s1_in[target].astype(F32)

    def distance(i):
        half = nz // 2
        middle = jnp.where(i < half, i, i + 1)
        return jnp.where(i == 0, half % nz, jnp.where(i == nz - 1, 0, middle))

    def give(i, d_y):
        target = other_z(distance(i)) * ny + other_y(d_y)
        s1_out[target] = partial_for(target * 2 + 1 - c).astype(BF16)
        s1_copy(target).start()

    def keep(i, d_y):
        target = other_z(distance(i)) * ny + other_y(d_y)
        acc[target] = partial_for(target * 2 + c)

    def step_two(i, d_y):
        d = distance(i)
        keep(i, d_y)
        s2_out[d, d_y] = chip_sum(other_z(d) * ny + other_y(d_y)).astype(BF16)
        s2_copy(d, d_y).start()

    def column_sum(d):
        total = chip_sum(other_z(d) * ny + y)
        for d_y in range(1, ny):
            s2_copy(d, d_y).wait_recv()
            total = total + s2_in[d, d_y].astype(F32)
        return total

    def step_three(i):
        d = distance(i)
        s3_out[d] = column_sum(d).astype(BF16)
        s3_copy(d).start()

    for d_y in range(1, ny):
        each(0, nz, functools.partial(give, d_y=d_y))
    for d_y in range(1, ny):
        each(0, nz, functools.partial(step_two, d_y=d_y))
    each(0, nz, functools.partial(give, d_y=0))
    each(0, nz, functools.partial(keep, d_y=0))
    each(0, nz - 1, step_three)
    acc[chip] = column_sum(0)

    def last(d):
        s3_copy(d).wait_recv()
        acc[chip] += s3_in[d].astype(F32)

    each(1, nz, last)
    out[...] = acc[chip].astype(out.dtype)

    def tok_sent(i):
        d = i // chunks
        k = lax.rem(i, chunks)

        @pl.when((z - d >= 0) & (z + 1 < nz))
        def _():
            tok_z(seq_of(z - d, y, c), k, d, True).wait_send()

        @pl.when((z + d < nz) & (z >= 1))
        def _():
            tok_z(seq_of(z + d, y, c), k, d, False).wait_send()

        for d_y in range(1, ny):
            tok_y(me, k, d, d_y).wait_send()

    each(0, nz * chunks, tok_sent)
    each(0, chips * chunks, lambda i: tok_c(
        (i // chunks) * 2 + c, lax.rem(i, chunks)).wait_send())
    each(1, n, lambda i: gain_copy(i).wait_send())
    each(1, chips, lambda i: k_copy(i).wait_send())
    each(1, chips, lambda i: v_copy(i).wait_send())

    def core_sent(i):
        slot = i * 2 + c
        kv_pair(k_buf.at[slot], k_buf, k_send_c, k_recv, slot).wait_send()
        kv_pair(v_buf.at[slot], v_buf, v_send_c, v_recv, slot).wait_send()
        s1_copy(i).wait_send()

    each(0, chips, core_sent)
    for i in range(1, members):
        own_copy(0, k_own, i).wait_send()
        own_copy(1, v_own, i).wait_send()
    for d_y in range(1, ny):
        each(0, nz, lambda d, d_y=d_y: s2_copy(d, d_y).wait_send())
    each(1, nz, lambda d: s3_copy(d).wait_send())


def body(n, ny, tokens, gain, w_query, w_key, w_value, w_out, cache):
    rows, width = tokens.shape
    features = w_query.shape[1]
    heads = H // n
    chips = n // 2
    nz = chips // ny
    members = n // KV
    own = w_key.shape[0]
    positions = cache.shape[1]
    stack = heads * rows
    dma = pltpu.SemaphoreType.DMA
    hbm = pl.BlockSpec(memory_space=pl.ANY)
    vmem = pl.BlockSpec(memory_space=pltpu.VMEM)
    block = (rows, width)
    return pl.pallas_call(
        functools.partial(kernel, n, ny),
        out_shape=jax.ShapeDtypeStruct((rows, width), BF16),
        in_specs=[vmem, vmem, hbm, hbm, hbm, hbm, hbm],
        out_specs=vmem,
        scratch_shapes=[
            pltpu.VMEM((n, rows, width), BF16),
            pltpu.VMEM((1, width), F32),
            pltpu.VMEM((n, 1, width), F32),
            pltpu.VMEM((rows, features), BF16),
            pltpu.VMEM(w_query.shape, BF16),
            pltpu.VMEM(w_key.shape, BF16),
            pltpu.VMEM(w_value.shape, BF16),
            pltpu.VMEM(w_out.shape, BF16),
            pltpu.VMEM((rows, heads * DH), F32),
            pltpu.VMEM((own, rows), F32),
            pltpu.VMEM((own, rows), F32),
            pltpu.VMEM((stack, DH), BF16),
            pltpu.VMEM((members, own, rows), BF16),
            pltpu.VMEM((members, own, rows), BF16),
            pltpu.VMEM((n, positions, DH), BF16),
            pltpu.VMEM((n, positions, DH), BF16),
            pltpu.VMEM((n, stack, positions), F32),
            pltpu.VMEM((stack, 128), F32),
            pltpu.VMEM((stack, 128), F32),
            pltpu.VMEM((stack, DH), F32),
            pltpu.VMEM((rows, heads * DH), BF16),
            pltpu.VMEM((chips,) + block, F32),
            pltpu.VMEM((chips,) + block, BF16),
            pltpu.VMEM((chips,) + block, BF16),
            pltpu.VMEM((nz, ny) + block, BF16),
            pltpu.VMEM((nz, ny) + block, BF16),
            pltpu.VMEM((nz,) + block, BF16),
            pltpu.VMEM((nz,) + block, BF16),
            dma((8,)),
            dma((n,)), dma((n,)),
            dma((nz, CHUNKS)), dma((nz, CHUNKS)), dma((nz, ny, CHUNKS)), dma((chips, CHUNKS)),
            dma((n, CHUNKS)),
            dma((chips,)), dma((chips,)), dma((n,)),
            dma((chips,)), dma((chips,)), dma((n,)),
            dma((2, members)), dma((2, members)),
            dma((chips,)), dma((chips,)),
            dma((nz, ny)), dma((nz, ny)),
            dma((nz,)), dma((nz,)),
        ],
        compiler_params=pltpu.CompilerParams(
            collective_id=0, has_side_effects=True, vmem_limit_bytes=60 * 2**20
        ),
    )(tokens, gain, w_query, w_key, w_value, w_out, cache)


def solution(mesh):
    n = mesh.shape["seq"]
    ny = max(1, 4 // mesh.shape["group"])
    return jax.shard_map(
        functools.partial(body, n, ny),
        mesh=mesh,
        in_specs=(
            P("group", "seq"),
            P("seq"),
            P("seq", None),
            P("seq", None),
            P("seq", None),
            P("seq", None),
            P(None, ("group", "seq"), None),
        ),
        out_specs=P("group", "seq"),
        check_vma=False,
    )
```

```python
import functools
import math

import jax
import jax.numpy as jnp
from jax import lax
from jax.experimental import pallas as pl
from jax.experimental.pallas import tpu as pltpu
from jax.sharding import PartitionSpec as P

H = 64
KV = 8
DH = 128
CHUNKS = 2
NT = (((1,), (1,)), ((), ()))
MESH = pl.DeviceIdType.MESH
F32 = jnp.float32
BF16 = jnp.bfloat16


def kernel(
    n, ny, tokens, gain_in, w_query, w_key, w_value, w_out, cache, out,
    tok, my_gain, gains, normed, wq, wk, wv, wo, q_acc, k_acc, v_acc, q_rows, k_own, v_own,
    k_buf, v_buf, scores, top, low, numer, att, acc, s1_out, s1_in, s2_out, s2_in, s3_out, s3_in,
    local_sem, gain_send, gain_recv, tok_up, tok_down, tok_send_y, tok_send_c, tok_recv,
    k_send, k_send_c, k_recv, v_send, v_send_c, v_recv, own_send, own_recv,
    s1_send, s1_recv, s2_send, s2_recv, s3_send, s3_recv,
):
    chips = n // 2
    nz = chips // ny
    me = lax.axis_index("seq")
    c = lax.rem(me, 2)
    chip = me // 2
    y = lax.rem(chip, ny)
    z = chip // ny
    partner = chip * 2 + 1 - c
    rows, width = tokens.shape
    heads = H // n
    members = n // KV
    kv_head = me // members
    member = lax.rem(me, members)
    positions = cache.shape[1]
    lanes = [slice(k * 128, (k + 1) * 128) for k in range(positions // 128)]
    scale = 1.0 / math.sqrt(DH)

    def seq_of(z_, y_, c_):
        return (z_ * ny + y_) * 2 + c_

    def other_z(d):
        return lax.rem(z + d, nz)

    def other_y(d):
        return lax.rem(y + d, ny)

    def remote(src, dst, send, recv, to):
        return pltpu.make_async_remote_copy(
            src_ref=src, dst_ref=dst, send_sem=send, recv_sem=recv,
            device_id={"seq": to}, device_id_type=MESH,
        )

    def each(start, stop, step):
        lax.fori_loop(start, stop, lambda i, carry: (step(i), carry)[1], 0)

    weights_in = [
        pltpu.make_async_copy(src, dst, local_sem.at[i])
        for i, (src, dst) in enumerate(
            [(w_query, wq), (w_key, wk), (w_value, wv), (w_out, wo)]
        )
    ]
    own_tok = pltpu.make_async_copy(tokens, tok.at[me], local_sem.at[4])
    gain = my_gain
    my_gain[...] = gain_in[...].astype(F32).reshape(1, width)
    gains[me] = my_gain[...]

    def own_cols(to_kv):
        return pl.ds(pl.multiple_of(to_kv * DH, DH), DH)

    own_k = pltpu.make_async_copy(
        cache.at[0, :, own_cols(kv_head)], k_buf.at[me], local_sem.at[6]
    )
    own_v = pltpu.make_async_copy(
        cache.at[1, :, own_cols(kv_head)], v_buf.at[me], local_sem.at[7]
    )
    for copy in weights_in:
        copy.start()
    own_tok.start()

    barrier = pltpu.get_barrier_semaphore()

    def greet(to):
        pl.semaphore_signal(barrier, inc=1, device_id={"seq": to}, device_id_type=MESH)

    @pl.when(z >= 1)
    def _():
        greet(seq_of(z - 1, y, c))

    @pl.when(z + 1 < nz)
    def _():
        greet(seq_of(z + 1, y, c))

    for d_y in range(1, ny):
        greet(seq_of(z, other_y(d_y), c))
    greet(partner)
    pl.semaphore_wait(
        barrier, ny + jnp.where(z >= 1, 1, 0) + jnp.where(z + 1 < nz, 1, 0))

    chunks = tok_recv.shape[1]
    deep = rows // chunks

    def piece_of(slot, k):
        return tok.at[slot, pl.ds(pl.multiple_of(k * deep, deep), deep), :]

    def tok_z(slot, k, d, up):
        ends = tok_up if up else tok_down
        to = jnp.clip(z + (1 if up else -1), 0, nz - 1)
        return remote(piece_of(slot, k), piece_of(slot, k), ends.at[d, k],
                      tok_recv.at[slot, k], seq_of(to, y, c))

    def tok_y(slot, k, d_z, d_y):
        return remote(piece_of(slot, k), piece_of(slot, k), tok_send_y.at[d_z, d_y, k],
                      tok_recv.at[slot, k], seq_of(z, other_y(d_y), c))

    def tok_c(slot, k):
        return remote(piece_of(slot, k), piece_of(slot, k), tok_send_c.at[slot // 2, k],
                      tok_recv.at[slot, k], partner)

    def tok_wait(slot, k):
        remote(piece_of(slot, k), piece_of(slot, k), tok_send_c.at[0, k], tok_recv.at[slot, k],
               partner).wait_recv()

    own_tok.wait()

    def send_own(k):
        @pl.when(z + 1 < nz)
        def _():
            tok_z(me, k, 0, True).start()

        @pl.when(z >= 1)
        def _():
            tok_z(me, k, 0, False).start()

        for d_y in range(1, ny):
            tok_y(me, k, z, d_y).start()
        tok_c(me, k).start()

    each(0, chunks, send_own)

    def gain_copy(i):
        return remote(gain, gains.at[me], gain_send.at[i], gain_recv.at[me],
                      lax.rem(chip + i, chips) * 2 + c)

    def gain_pair(i):
        slot = lax.rem(chip + i, chips) * 2 + c
        return remote(gains.at[slot], gains.at[slot], gain_send.at[chips + i],
                      gain_recv.at[slot], partner)

    def kv_copy(half, buf, send, recv, i):
        other = lax.rem(chip + i, chips)
        to = other * 2 + c
        return remote(cache.at[half, :, own_cols(to // members)], buf.at[me], send.at[i],
                      recv.at[me], to)

    def kv_pair(src, buf, send, recv, slot):
        return remote(src, buf.at[slot], send.at[slot // 2], recv.at[slot], partner)

    def kv_wait(buf, send, recv, slot):
        remote(buf.at[slot], buf.at[slot], send.at[0], recv.at[slot], partner).wait_recv()

    def k_copy(i):
        return kv_copy(0, k_buf, k_send, k_recv, i)

    def v_copy(i):
        return kv_copy(1, v_buf, v_send, v_recv, i)


    def forward_z(i):
        d = 1 + i // chunks
        k = lax.rem(i, chunks)

        def pass_on(slot, up):
            tok_wait(slot, k)

            @pl.when((z + 1 < nz) if up else (z >= 1))
            def _():
                tok_z(slot, k, d, up).start()

            for d_y in range(1, ny):
                tok_y(slot, k, slot // (2 * ny), d_y).start()
            tok_c(slot, k).start()

        @pl.when(z - d >= 0)
        def _():
            pass_on(seq_of(z - d, y, c), True)

        @pl.when(z + d < nz)
        def _():
            pass_on(seq_of(z + d, y, c), False)

    each(0, (nz - 1) * chunks, forward_z)
    each(1, chips, lambda i: gain_copy(i).start())
    gain_pair(0).start()
    each(1, chips, lambda i: k_copy(i).start())
    k_own_src = cache.at[0, :, own_cols(kv_head)]
    v_own_src = cache.at[1, :, own_cols(kv_head)]
    kv_pair(k_own_src, k_buf, k_send_c, k_recv, me).start()
    own_k.start()


    def spread(i):
        reach = jnp.minimum(z, nz - 1 - z)
        side = jnp.where(lax.rem(i, 2) == 1, z - (i + 1) // 2, z + i // 2)
        return jnp.where(i <= 2 * reach, side, jnp.where(z < nz - 1 - z, i, nz - 1 - i))

    for d_y in range(1, ny):
        def forward_y(i, d_y=d_y):
            there = seq_of(spread(i // chunks), other_y(d_y), c)
            k = lax.rem(i, chunks)
            tok_wait(there, k)
            tok_c(there, k).start()
        each(0, nz * chunks, forward_y)

    each(1, chips, lambda i: v_copy(i).start())

    def gain_wait(slot):
        remote(gain, gains.at[slot], gain_send.at[0], gain_recv.at[slot], partner).wait_recv()

    def gain_step(i):
        gain_wait(lax.rem(chip + i, chips) * 2 + c)
        gain_pair(i).start()

    each(1, chips, gain_step)
    kv_pair(v_own_src, v_buf, v_send_c, v_recv, me).start()
    own_v.start()

    each(0, chips * chunks, lambda i: tok_wait((i // chunks) * 2 + 1 - c, lax.rem(i, chunks)))

    parts = width // 128

    def square_step(b, total):
        x = tok[b].astype(F32)
        for k in range(parts):
            piece = x[:, k * 128:(k + 1) * 128]
            total = total + piece * piece
        return total

    total = lax.fori_loop(0, n, square_step, jnp.zeros((rows, 128), F32))
    each(0, chips, lambda i: gain_wait(i * 2 + 1 - c))
    mean = jnp.sum(total, axis=1, keepdims=True) * (1.0 / (n * width))
    inverse = jnp.broadcast_to(lax.rsqrt(mean + 1e-05), (rows, 128))

    def norm_step(b):
        for k in range(parts):
            x = tok[b, :, k * 128:(k + 1) * 128].astype(F32)
            g = gains[b, :, k * 128:(k + 1) * 128].astype(F32)
            normed[:, pl.ds(pl.multiple_of(b * width + k * 128, 128), 128)] = (
                x * inverse * g).astype(BF16)

    each(0, n, norm_step)

    for copy in weights_in[:3]:
        copy.wait()
    q_acc[...] = jnp.zeros_like(q_acc)
    k_acc[...] = jnp.zeros_like(k_acc)
    v_acc[...] = jnp.zeros_like(v_acc)
    depth = 1024

    def project(i):
        cols = pl.ds(pl.multiple_of(i * depth, depth), depth)
        x = normed[:, cols]
        k_acc[...] += lax.dot_general(wk[:, cols], x, NT, preferred_element_type=F32)
        v_acc[...] += lax.dot_general(wv[:, cols], x, NT, preferred_element_type=F32)
        q_acc[...] += lax.dot_general(x, wq[:, cols], NT, preferred_element_type=F32)

    each(0, normed.shape[1] // depth, project)
    k_own[member] = k_acc[...].astype(BF16)
    v_own[member] = v_acc[...].astype(BF16)

    def own_copy(which, buf, i):
        return remote(buf.at[member], buf.at[member], own_send.at[which, i],
                      own_recv.at[which, member], kv_head * members + lax.rem(member + i, members))

    def own_wait(which, buf, i):
        slot = lax.rem(member + i, members)
        remote(buf.at[slot], buf.at[slot], own_send.at[which, 0], own_recv.at[which, slot],
               partner).wait_recv()

    for i in range(1, members):
        own_copy(0, k_own, i).start()
        own_copy(1, v_own, i).start()

    for h in range(heads):
        q_rows[h * rows:(h + 1) * rows, :] = q_acc[:, h * DH:(h + 1) * DH].astype(BF16)

    top[...] = jnp.full_like(top, -jnp.inf)

    def score_block(slot):
        keys = k_buf[slot]
        for h in range(heads):
            here = slice(h * rows, (h + 1) * rows)
            s = lax.dot_general(q_rows[here, :], keys, NT, preferred_element_type=F32) * scale
            scores[slot, here, :] = s
            best = top[here, :]
            for part in lanes:
                best = jnp.maximum(best, s[:, part])
            top[here, :] = best

    own_k.wait()
    score_block(me)

    def k_mine(i):
        slot = lax.rem(chip + chips - i, chips) * 2 + c
        kv_wait(k_buf, k_send_c, k_recv, slot)
        kv_pair(k_buf.at[slot], k_buf, k_send_c, k_recv, slot).start()
        score_block(slot)

    each(1, chips, k_mine)

    def k_theirs(i):
        slot = lax.rem(chip + chips - i, chips) * 2 + 1 - c
        kv_wait(k_buf, k_send_c, k_recv, slot)
        score_block(slot)

    each(0, chips, k_theirs)

    for i in range(1, members):
        own_wait(0, k_own, i)
        own_wait(1, v_own, i)
    key_rows = k_own[...].astype(F32).reshape(DH, rows).T
    own_scores = []
    for h in range(heads):
        here = slice(h * rows, (h + 1) * rows)
        own = jnp.sum(q_rows[here, :].astype(F32) * key_rows, axis=1, keepdims=True) * scale
        best = jnp.maximum(jnp.max(top[here, :], axis=1, keepdims=True), own)
        top[here, :] = jnp.broadcast_to(best, (rows, 128))
        own_scores.append(jnp.exp(own - best))

    low[...] = jnp.zeros_like(low)
    numer[...] = jnp.zeros_like(numer)

    def value_block(slot):
        values = v_buf[slot]
        for h in range(heads):
            here = slice(h * rows, (h + 1) * rows)
            best = top[here, :]
            pieces = [jnp.exp(scores[slot, here, part] - best) for part in lanes]
            low[here, :] += functools.reduce(jnp.add, pieces)
            weights = jnp.concatenate([piece.astype(BF16) for piece in pieces], axis=1)
            numer[here, :] += jnp.dot(weights, values, preferred_element_type=F32)

    own_v.wait()
    value_block(me)

    def v_mine(i):
        slot = lax.rem(chip + chips - i, chips) * 2 + c
        kv_wait(v_buf, v_send_c, v_recv, slot)
        kv_pair(v_buf.at[slot], v_buf, v_send_c, v_recv, slot).start()
        value_block(slot)

    each(1, chips, v_mine)

    def v_theirs(i):
        slot = lax.rem(chip + chips - i, chips) * 2 + 1 - c
        kv_wait(v_buf, v_send_c, v_recv, slot)
        value_block(slot)

    each(0, chips, v_theirs)

    value_rows = v_own[...].astype(F32).reshape(DH, rows).T
    for h in range(heads):
        here = slice(h * rows, (h + 1) * rows)
        own_weight = own_scores[h]
        denom = jnp.sum(low[here, :], axis=1, keepdims=True) + own_weight
        total = numer[here, :] + own_weight.astype(BF16).astype(F32) * value_rows
        att[:, h * DH:(h + 1) * DH] = (total / denom).astype(BF16)

    weights_in[3].wait()

    def partial_for(to):
        cols = pl.ds(pl.multiple_of(to * width, width), width)
        return jnp.dot(att[...], wo[:, cols], preferred_element_type=F32)

    def s1_copy(target):
        return remote(s1_out.at[target], s1_in.at[target], s1_send.at[target],
                      s1_recv.at[target], partner)

    def s2_copy(d_z, d_y):
        return remote(s2_out.at[d_z, d_y], s2_in.at[d_z, d_y], s2_send.at[d_z, d_y],
                      s2_recv.at[d_z, d_y], seq_of(z, other_y(d_y), c))

    def s3_copy(d):
        return remote(s3_out.at[d], s3_in.at[d], s3_send.at[d], s3_recv.at[d],
                      seq_of(other_z(d), y, c))

    def chip_sum(target):
        s1_copy(target).wait_recv()
        return acc[target] + s1_in[target].astype(F32)

    def distance(i):
        half = nz // 2
        middle = jnp.where(i < half, i, i + 1)
        return jnp.where(i == 0, half % nz, jnp.where(i == nz - 1, 0, middle))

    def give(i, d_y):
        target = other_z(distance(i)) * ny + other_y(d_y)
        s1_out[target] = partial_for(target * 2 + 1 - c).astype(BF16)
        s1_copy(target).start()

    def keep(i, d_y):
        target = other_z(distance(i)) * ny + other_y(d_y)
        acc[target] = partial_for(target * 2 + c)

    def step_two(i, d_y):
        d = distance(i)
        keep(i, d_y)
        s2_out[d, d_y] = chip_sum(other_z(d) * ny + other_y(d_y)).astype(BF16)
        s2_copy(d, d_y).start()

    def column_sum(d):
        total = chip_sum(other_z(d) * ny + y)
        for d_y in range(1, ny):
            s2_copy(d, d_y).wait_recv()
            total = total + s2_in[d, d_y].astype(F32)
        return total

    def step_three(i):
        d = distance(i)
        s3_out[d] = column_sum(d).astype(BF16)
        s3_copy(d).start()

    for d_y in range(1, ny):
        each(0, nz, functools.partial(give, d_y=d_y))
    for d_y in range(1, ny):
        each(0, nz, functools.partial(step_two, d_y=d_y))
    each(0, nz, functools.partial(give, d_y=0))
    each(0, nz, functools.partial(keep, d_y=0))
    each(0, nz - 1, step_three)
    acc[chip] = column_sum(0)

    def last(d):
        s3_copy(d).wait_recv()
        acc[chip] += s3_in[d].astype(F32)

    each(1, nz, last)
    out[...] = acc[chip].astype(out.dtype)

    def tok_sent(i):
        d = i // chunks
        k = lax.rem(i, chunks)

        @pl.when((z - d >= 0) & (z + 1 < nz))
        def _():
            tok_z(seq_of(z - d, y, c), k, d, True).wait_send()

        @pl.when((z + d < nz) & (z >= 1))
        def _():
            tok_z(seq_of(z + d, y, c), k, d, False).wait_send()

        for d_y in range(1, ny):
            tok_y(me, k, d, d_y).wait_send()

    each(0, nz * chunks, tok_sent)
    each(0, chips * chunks, lambda i: tok_c(
        (i // chunks) * 2 + c, lax.rem(i, chunks)).wait_send())
    each(1, chips, lambda i: gain_copy(i).wait_send())
    each(0, chips, lambda i: gain_pair(i).wait_send())
    each(1, chips, lambda i: k_copy(i).wait_send())
    each(1, chips, lambda i: v_copy(i).wait_send())

    def core_sent(i):
        slot = i * 2 + c
        kv_pair(k_buf.at[slot], k_buf, k_send_c, k_recv, slot).wait_send()
        kv_pair(v_buf.at[slot], v_buf, v_send_c, v_recv, slot).wait_send()
        s1_copy(i).wait_send()

    each(0, chips, core_sent)
    for i in range(1, members):
        own_copy(0, k_own, i).wait_send()
        own_copy(1, v_own, i).wait_send()
    for d_y in range(1, ny):
        each(0, nz, lambda d, d_y=d_y: s2_copy(d, d_y).wait_send())
    each(1, nz, lambda d: s3_copy(d).wait_send())


def body(n, ny, tokens, gain, w_query, w_key, w_value, w_out, cache):
    rows, width = tokens.shape
    features = w_query.shape[1]
    heads = H // n
    chips = n // 2
    nz = chips // ny
    members = n // KV
    own = w_key.shape[0]
    positions = cache.shape[1]
    stack = heads * rows
    dma = pltpu.SemaphoreType.DMA
    hbm = pl.BlockSpec(memory_space=pl.ANY)
    vmem = pl.BlockSpec(memory_space=pltpu.VMEM)
    block = (rows, width)
    return pl.pallas_call(
        functools.partial(kernel, n, ny),
        out_shape=jax.ShapeDtypeStruct((rows, width), BF16),
        in_specs=[vmem, vmem, hbm, hbm, hbm, hbm, hbm],
        out_specs=vmem,
        scratch_shapes=[
            pltpu.VMEM((n, rows, width), BF16),
            pltpu.VMEM((1, width), F32),
            pltpu.VMEM((n, 1, width), F32),
            pltpu.VMEM((rows, features), BF16),
            pltpu.VMEM(w_query.shape, BF16),
            pltpu.VMEM(w_key.shape, BF16),
            pltpu.VMEM(w_value.shape, BF16),
            pltpu.VMEM(w_out.shape, BF16),
            pltpu.VMEM((rows, heads * DH), F32),
            pltpu.VMEM((own, rows), F32),
            pltpu.VMEM((own, rows), F32),
            pltpu.VMEM((stack, DH), BF16),
            pltpu.VMEM((members, own, rows), BF16),
            pltpu.VMEM((members, own, rows), BF16),
            pltpu.VMEM((n, positions, DH), BF16),
            pltpu.VMEM((n, positions, DH), BF16),
            pltpu.VMEM((n, stack, positions), F32),
            pltpu.VMEM((stack, 128), F32),
            pltpu.VMEM((stack, 128), F32),
            pltpu.VMEM((stack, DH), F32),
            pltpu.VMEM((rows, heads * DH), BF16),
            pltpu.VMEM((chips,) + block, F32),
            pltpu.VMEM((chips,) + block, BF16),
            pltpu.VMEM((chips,) + block, BF16),
            pltpu.VMEM((nz, ny) + block, BF16),
            pltpu.VMEM((nz, ny) + block, BF16),
            pltpu.VMEM((nz,) + block, BF16),
            pltpu.VMEM((nz,) + block, BF16),
            dma((8,)),
            dma((n,)), dma((n,)),
            dma((nz, CHUNKS)), dma((nz, CHUNKS)), dma((nz, ny, CHUNKS)), dma((chips, CHUNKS)),
            dma((n, CHUNKS)),
            dma((chips,)), dma((chips,)), dma((n,)),
            dma((chips,)), dma((chips,)), dma((n,)),
            dma((2, members)), dma((2, members)),
            dma((chips,)), dma((chips,)),
            dma((nz, ny)), dma((nz, ny)),
            dma((nz,)), dma((nz,)),
        ],
        compiler_params=pltpu.CompilerParams(
            collective_id=0, has_side_effects=True, vmem_limit_bytes=60 * 2**20
        ),
    )(tokens, gain, w_query, w_key, w_value, w_out, cache)


def solution(mesh):
    n = mesh.shape["seq"]
    ny = max(1, 4 // mesh.shape["group"])
    return jax.shard_map(
        functools.partial(body, n, ny),
        mesh=mesh,
        in_specs=(
            P("group", "seq"),
            P("seq"),
            P("seq", None),
            P("seq", None),
            P("seq", None),
            P("seq", None),
            P(None, ("group", "seq"), None),
        ),
        out_specs=P("group", "seq"),
        check_vma=False,
    )
```

```python
import functools
import math

import jax
import jax.numpy as jnp
from jax import lax
from jax.experimental import pallas as pl
from jax.experimental.pallas import tpu as pltpu
from jax.sharding import PartitionSpec as P

H = 64
KV = 8
DH = 128
CHUNKS = 2
CUTS = 2
NT = (((1,), (1,)), ((), ()))
MESH = pl.DeviceIdType.MESH
F32 = jnp.float32
BF16 = jnp.bfloat16


def kernel(
    n, ny, tokens, gain_in, w_query, w_key, w_value, w_out, cache, out,
    tok, my_gain, gains, normed, wq, wk, wv, wo, q_acc, k_acc, v_acc, q_rows, k_own, v_own,
    k_buf, v_buf, scores, top, low, numer, att, acc, s1_out, s1_in, s2_out, s2_in, s3_out, s3_in,
    local_sem, gain_send, gain_recv, tok_up, tok_down, tok_send_y, tok_send_c, tok_recv,
    k_send, k_send_c, k_recv, v_send, v_send_c, v_recv, own_send, own_recv,
    s1_send, s1_recv, s2_send, s2_recv, s3_send, s3_recv,
):
    chips = n // 2
    nz = chips // ny
    me = lax.axis_index("seq")
    c = lax.rem(me, 2)
    chip = me // 2
    y = lax.rem(chip, ny)
    z = chip // ny
    partner = chip * 2 + 1 - c
    rows, width = tokens.shape
    heads = H // n
    members = n // KV
    kv_head = me // members
    member = lax.rem(me, members)
    positions = cache.shape[1]
    lanes = [slice(k * 128, (k + 1) * 128) for k in range(positions // 128)]
    scale = 1.0 / math.sqrt(DH)

    def seq_of(z_, y_, c_):
        return (z_ * ny + y_) * 2 + c_

    def other_z(d):
        return lax.rem(z + d, nz)

    def other_y(d):
        return lax.rem(y + d, ny)

    def remote(src, dst, send, recv, to):
        return pltpu.make_async_remote_copy(
            src_ref=src, dst_ref=dst, send_sem=send, recv_sem=recv,
            device_id={"seq": to}, device_id_type=MESH,
        )

    def each(start, stop, step):
        lax.fori_loop(start, stop, lambda i, carry: (step(i), carry)[1], 0)

    weights_in = [
        pltpu.make_async_copy(src, dst, local_sem.at[i])
        for i, (src, dst) in enumerate(
            [(w_query, wq), (w_key, wk), (w_value, wv), (w_out, wo)]
        )
    ]
    own_tok = pltpu.make_async_copy(tokens, tok.at[me], local_sem.at[4])
    gain = my_gain
    my_gain[...] = gain_in[...].astype(F32).reshape(1, width)
    gains[me] = my_gain[...]

    def own_cols(to_kv):
        return pl.ds(pl.multiple_of(to_kv * DH, DH), DH)

    own_k = pltpu.make_async_copy(
        cache.at[0, :, own_cols(kv_head)], k_buf.at[me], local_sem.at[6]
    )
    own_v = pltpu.make_async_copy(
        cache.at[1, :, own_cols(kv_head)], v_buf.at[me], local_sem.at[7]
    )
    for copy in weights_in:
        copy.start()
    own_tok.start()

    barrier = pltpu.get_barrier_semaphore()

    def greet(to):
        pl.semaphore_signal(barrier, inc=1, device_id={"seq": to}, device_id_type=MESH)

    @pl.when(z >= 1)
    def _():
        greet(seq_of(z - 1, y, c))

    @pl.when(z + 1 < nz)
    def _():
        greet(seq_of(z + 1, y, c))

    for d_y in range(1, ny):
        greet(seq_of(z, other_y(d_y), c))
    greet(partner)
    pl.semaphore_wait(
        barrier, ny + jnp.where(z >= 1, 1, 0) + jnp.where(z + 1 < nz, 1, 0))

    chunks = tok_recv.shape[1]
    deep = rows // chunks

    def piece_of(slot, k):
        return tok.at[slot, pl.ds(pl.multiple_of(k * deep, deep), deep), :]

    def tok_z(slot, k, d, up):
        ends = tok_up if up else tok_down
        to = jnp.clip(z + (1 if up else -1), 0, nz - 1)
        return remote(piece_of(slot, k), piece_of(slot, k), ends.at[d, k],
                      tok_recv.at[slot, k], seq_of(to, y, c))

    def tok_y(slot, k, d_z, d_y):
        return remote(piece_of(slot, k), piece_of(slot, k), tok_send_y.at[d_z, d_y, k],
                      tok_recv.at[slot, k], seq_of(z, other_y(d_y), c))

    def tok_c(slot, k):
        return remote(piece_of(slot, k), piece_of(slot, k), tok_send_c.at[slot // 2, k],
                      tok_recv.at[slot, k], partner)

    def tok_wait(slot, k):
        remote(piece_of(slot, k), piece_of(slot, k), tok_send_c.at[0, k], tok_recv.at[slot, k],
               partner).wait_recv()

    own_tok.wait()

    def send_own(k):
        @pl.when(z + 1 < nz)
        def _():
            tok_z(me, k, 0, True).start()

        @pl.when(z >= 1)
        def _():
            tok_z(me, k, 0, False).start()

        for d_y in range(1, ny):
            tok_y(me, k, z, d_y).start()
        tok_c(me, k).start()

    each(0, chunks, send_own)

    def gain_copy(i):
        return remote(gain, gains.at[me], gain_send.at[i], gain_recv.at[me],
                      lax.rem(chip + i, chips) * 2 + c)

    def gain_pair(i):
        slot = lax.rem(chip + i, chips) * 2 + c
        return remote(gains.at[slot], gains.at[slot], gain_send.at[chips + i],
                      gain_recv.at[slot], partner)

    def kv_copy(half, buf, send, recv, i):
        other = lax.rem(chip + i, chips)
        to = other * 2 + c
        return remote(cache.at[half, :, own_cols(to // members)], buf.at[me], send.at[i],
                      recv.at[me], to)

    def kv_pair(src, buf, send, recv, slot):
        return remote(src, buf.at[slot], send.at[slot // 2], recv.at[slot], partner)

    def kv_wait(buf, send, recv, slot):
        remote(buf.at[slot], buf.at[slot], send.at[0], recv.at[slot], partner).wait_recv()

    def k_copy(i):
        return kv_copy(0, k_buf, k_send, k_recv, i)

    def v_copy(i):
        return kv_copy(1, v_buf, v_send, v_recv, i)


    def forward_z(i):
        d = 1 + i // chunks
        k = lax.rem(i, chunks)

        def pass_on(slot, up):
            tok_wait(slot, k)

            @pl.when((z + 1 < nz) if up else (z >= 1))
            def _():
                tok_z(slot, k, d, up).start()

            for d_y in range(1, ny):
                tok_y(slot, k, slot // (2 * ny), d_y).start()
            tok_c(slot, k).start()

        @pl.when(z - d >= 0)
        def _():
            pass_on(seq_of(z - d, y, c), True)

        @pl.when(z + d < nz)
        def _():
            pass_on(seq_of(z + d, y, c), False)

    each(0, (nz - 1) * chunks, forward_z)
    each(1, chips, lambda i: gain_copy(i).start())
    gain_pair(0).start()
    each(1, chips, lambda i: k_copy(i).start())
    k_own_src = cache.at[0, :, own_cols(kv_head)]
    v_own_src = cache.at[1, :, own_cols(kv_head)]
    kv_pair(k_own_src, k_buf, k_send_c, k_recv, me).start()
    own_k.start()


    def spread(i):
        reach = jnp.minimum(z, nz - 1 - z)
        side = jnp.where(lax.rem(i, 2) == 1, z - (i + 1) // 2, z + i // 2)
        return jnp.where(i <= 2 * reach, side, jnp.where(z < nz - 1 - z, i, nz - 1 - i))

    for d_y in range(1, ny):
        def forward_y(i, d_y=d_y):
            there = seq_of(spread(i // chunks), other_y(d_y), c)
            k = lax.rem(i, chunks)
            tok_wait(there, k)
            tok_c(there, k).start()
        each(0, nz * chunks, forward_y)

    each(1, chips, lambda i: v_copy(i).start())

    def gain_wait(slot):
        remote(gain, gains.at[slot], gain_send.at[0], gain_recv.at[slot], partner).wait_recv()

    def gain_step(i):
        gain_wait(lax.rem(chip + i, chips) * 2 + c)
        gain_pair(i).start()

    each(1, chips, gain_step)
    kv_pair(v_own_src, v_buf, v_send_c, v_recv, me).start()
    own_v.start()

    each(0, chips * chunks, lambda i: tok_wait((i // chunks) * 2 + 1 - c, lax.rem(i, chunks)))

    parts = width // 128

    def square_step(b, total):
        x = tok[b].astype(F32)
        for k in range(parts):
            piece = x[:, k * 128:(k + 1) * 128]
            total = total + piece * piece
        return total

    total = lax.fori_loop(0, n, square_step, jnp.zeros((rows, 128), F32))
    each(0, chips, lambda i: gain_wait(i * 2 + 1 - c))
    mean = jnp.sum(total, axis=1, keepdims=True) * (1.0 / (n * width))
    inverse = jnp.broadcast_to(lax.rsqrt(mean + 1e-05), (rows, 128))

    def norm_step(b):
        for k in range(parts):
            x = tok[b, :, k * 128:(k + 1) * 128].astype(F32)
            g = gains[b, :, k * 128:(k + 1) * 128].astype(F32)
            normed[:, pl.ds(pl.multiple_of(b * width + k * 128, 128), 128)] = (
                x * inverse * g).astype(BF16)

    each(0, n, norm_step)

    for copy in weights_in[:3]:
        copy.wait()
    q_acc[...] = jnp.zeros_like(q_acc)
    k_acc[...] = jnp.zeros_like(k_acc)
    v_acc[...] = jnp.zeros_like(v_acc)
    depth = 1024

    def project(i):
        cols = pl.ds(pl.multiple_of(i * depth, depth), depth)
        x = normed[:, cols]
        k_acc[...] += lax.dot_general(wk[:, cols], x, NT, preferred_element_type=F32)
        v_acc[...] += lax.dot_general(wv[:, cols], x, NT, preferred_element_type=F32)
        q_acc[...] += lax.dot_general(x, wq[:, cols], NT, preferred_element_type=F32)

    each(0, normed.shape[1] // depth, project)
    k_own[member] = k_acc[...].astype(BF16)
    v_own[member] = v_acc[...].astype(BF16)

    def own_copy(which, buf, i):
        return remote(buf.at[member], buf.at[member], own_send.at[which, i],
                      own_recv.at[which, member], kv_head * members + lax.rem(member + i, members))

    def own_wait(which, buf, i):
        slot = lax.rem(member + i, members)
        remote(buf.at[slot], buf.at[slot], own_send.at[which, 0], own_recv.at[which, slot],
               partner).wait_recv()

    for i in range(1, members):
        own_copy(0, k_own, i).start()
        own_copy(1, v_own, i).start()

    for h in range(heads):
        q_rows[h * rows:(h + 1) * rows, :] = q_acc[:, h * DH:(h + 1) * DH].astype(BF16)

    top[...] = jnp.full_like(top, -jnp.inf)

    def score_block(slot):
        keys = k_buf[slot]
        for h in range(heads):
            here = slice(h * rows, (h + 1) * rows)
            s = lax.dot_general(q_rows[here, :], keys, NT, preferred_element_type=F32) * scale
            scores[slot, here, :] = s
            best = top[here, :]
            for part in lanes:
                best = jnp.maximum(best, s[:, part])
            top[here, :] = best

    own_k.wait()
    score_block(me)

    def k_mine(i):
        slot = lax.rem(chip + chips - i, chips) * 2 + c
        kv_wait(k_buf, k_send_c, k_recv, slot)
        kv_pair(k_buf.at[slot], k_buf, k_send_c, k_recv, slot).start()
        score_block(slot)

    each(1, chips, k_mine)

    def k_theirs(i):
        slot = lax.rem(chip + chips - i, chips) * 2 + 1 - c
        kv_wait(k_buf, k_send_c, k_recv, slot)
        score_block(slot)

    each(0, chips, k_theirs)

    for i in range(1, members):
        own_wait(0, k_own, i)
        own_wait(1, v_own, i)
    key_rows = k_own[...].astype(F32).reshape(DH, rows).T
    own_scores = []
    for h in range(heads):
        here = slice(h * rows, (h + 1) * rows)
        own = jnp.sum(q_rows[here, :].astype(F32) * key_rows, axis=1, keepdims=True) * scale
        best = jnp.maximum(jnp.max(top[here, :], axis=1, keepdims=True), own)
        top[here, :] = jnp.broadcast_to(best, (rows, 128))
        own_scores.append(jnp.exp(own - best))

    low[...] = jnp.zeros_like(low)
    numer[...] = jnp.zeros_like(numer)

    def value_block(slot):
        values = v_buf[slot]
        for h in range(heads):
            here = slice(h * rows, (h + 1) * rows)
            best = top[here, :]
            pieces = [jnp.exp(scores[slot, here, part] - best) for part in lanes]
            low[here, :] += functools.reduce(jnp.add, pieces)
            weights = jnp.concatenate([piece.astype(BF16) for piece in pieces], axis=1)
            numer[here, :] += jnp.dot(weights, values, preferred_element_type=F32)

    own_v.wait()
    value_block(me)

    def v_mine(i):
        slot = lax.rem(chip + chips - i, chips) * 2 + c
        kv_wait(v_buf, v_send_c, v_recv, slot)
        kv_pair(v_buf.at[slot], v_buf, v_send_c, v_recv, slot).start()
        value_block(slot)

    each(1, chips, v_mine)

    def v_theirs(i):
        slot = lax.rem(chip + chips - i, chips) * 2 + 1 - c
        kv_wait(v_buf, v_send_c, v_recv, slot)
        value_block(slot)

    each(0, chips, v_theirs)

    value_rows = v_own[...].astype(F32).reshape(DH, rows).T
    for h in range(heads):
        here = slice(h * rows, (h + 1) * rows)
        own_weight = own_scores[h]
        denom = jnp.sum(low[here, :], axis=1, keepdims=True) + own_weight
        total = numer[here, :] + own_weight.astype(BF16).astype(F32) * value_rows
        att[:, h * DH:(h + 1) * DH] = (total / denom).astype(BF16)

    weights_in[3].wait()

    def partial_for(to):
        cols = pl.ds(pl.multiple_of(to * width, width), width)
        return jnp.dot(att[...], wo[:, cols], preferred_element_type=F32)

    def s1_copy(target):
        return remote(s1_out.at[target], s1_in.at[target], s1_send.at[target],
                      s1_recv.at[target], partner)

    cuts = s2_send.shape[2]
    short = rows // cuts
    pieces = [slice(k * short, (k + 1) * short) for k in range(cuts)]

    def s2_copy(d_z, d_y, k):
        return remote(s2_out.at[d_z, d_y, pieces[k]], s2_in.at[d_z, d_y, pieces[k]],
                      s2_send.at[d_z, d_y, k], s2_recv.at[d_z, d_y, k], seq_of(z, other_y(d_y), c))

    def s3_copy(d, k):
        return remote(s3_out.at[d, pieces[k]], s3_in.at[d, pieces[k]], s3_send.at[d, k],
                      s3_recv.at[d, k], seq_of(other_z(d), y, c))

    def distance(i):
        down = nz - 1 - i
        down = jnp.where(down <= z, down - 1, down)
        up = jnp.where(i >= z, i + 1, i)
        there = jnp.where(z < nz - 1 - z, down, up)
        return lax.rem(jnp.where(i == nz - 1, z, there) - z + nz, nz)

    def give(i, d_y):
        target = other_z(distance(i)) * ny + other_y(d_y)
        s1_out[target] = partial_for(target * 2 + 1 - c).astype(BF16)
        s1_copy(target).start()

    def keep(i, d_y):
        target = other_z(distance(i)) * ny + other_y(d_y)
        acc[target] = partial_for(target * 2 + c)

    def step_two(i, d_y):
        d = distance(i)
        keep(i, d_y)
        target = other_z(d) * ny + other_y(d_y)
        s1_copy(target).wait_recv()
        for k, here in enumerate(pieces):
            s2_out[d, d_y, here, :] = (
                acc[target, here, :] + s1_in[target, here, :].astype(F32)).astype(BF16)
            s2_copy(d, d_y, k).start()

    def column_sum(d, k):
        here = pieces[k]
        target = other_z(d) * ny + y
        total = acc[target, here, :] + s1_in[target, here, :].astype(F32)
        for d_y in range(1, ny):
            s2_copy(d, d_y, k).wait_recv()
            total = total + s2_in[d, d_y, here, :].astype(F32)
        return total

    def step_three(i):
        d = distance(i)
        s1_copy(other_z(d) * ny + y).wait_recv()
        for k, here in enumerate(pieces):
            s3_out[d, here, :] = column_sum(d, k).astype(BF16)
            s3_copy(d, k).start()

    for d_y in range(1, ny):
        each(0, nz, functools.partial(give, d_y=d_y))
        each(0, nz, functools.partial(step_two, d_y=d_y))
    each(0, nz, functools.partial(give, d_y=0))
    each(0, nz, functools.partial(keep, d_y=0))
    each(0, nz - 1, step_three)
    s1_copy(chip).wait_recv()
    for k, here in enumerate(pieces):
        acc[chip, here, :] = column_sum(0, k)

    def last(d):
        for k, here in enumerate(pieces):
            s3_copy(d, k).wait_recv()
            acc[chip, here, :] += s3_in[d, here, :].astype(F32)

    each(1, nz, last)
    out[...] = acc[chip].astype(out.dtype)

    def tok_sent(i):
        d = i // chunks
        k = lax.rem(i, chunks)

        @pl.when((z - d >= 0) & (z + 1 < nz))
        def _():
            tok_z(seq_of(z - d, y, c), k, d, True).wait_send()

        @pl.when((z + d < nz) & (z >= 1))
        def _():
            tok_z(seq_of(z + d, y, c), k, d, False).wait_send()

        for d_y in range(1, ny):
            tok_y(me, k, d, d_y).wait_send()

    each(0, nz * chunks, tok_sent)
    each(0, chips * chunks, lambda i: tok_c(
        (i // chunks) * 2 + c, lax.rem(i, chunks)).wait_send())
    each(1, chips, lambda i: gain_copy(i).wait_send())
    each(0, chips, lambda i: gain_pair(i).wait_send())
    each(1, chips, lambda i: k_copy(i).wait_send())
    each(1, chips, lambda i: v_copy(i).wait_send())

    def core_sent(i):
        slot = i * 2 + c
        kv_pair(k_buf.at[slot], k_buf, k_send_c, k_recv, slot).wait_send()
        kv_pair(v_buf.at[slot], v_buf, v_send_c, v_recv, slot).wait_send()
        s1_copy(i).wait_send()

    each(0, chips, core_sent)
    for i in range(1, members):
        own_copy(0, k_own, i).wait_send()
        own_copy(1, v_own, i).wait_send()
    for d_y in range(1, ny):
        for k in range(cuts):
            each(0, nz, lambda d, d_y=d_y, k=k: s2_copy(d, d_y, k).wait_send())
    for k in range(cuts):
        each(1, nz, lambda d, k=k: s3_copy(d, k).wait_send())


def body(n, ny, tokens, gain, w_query, w_key, w_value, w_out, cache):
    rows, width = tokens.shape
    features = w_query.shape[1]
    heads = H // n
    chips = n // 2
    nz = chips // ny
    members = n // KV
    own = w_key.shape[0]
    positions = cache.shape[1]
    stack = heads * rows
    dma = pltpu.SemaphoreType.DMA
    hbm = pl.BlockSpec(memory_space=pl.ANY)
    vmem = pl.BlockSpec(memory_space=pltpu.VMEM)
    block = (rows, width)
    return pl.pallas_call(
        functools.partial(kernel, n, ny),
        out_shape=jax.ShapeDtypeStruct((rows, width), BF16),
        in_specs=[vmem, vmem, hbm, hbm, hbm, hbm, hbm],
        out_specs=vmem,
        scratch_shapes=[
            pltpu.VMEM((n, rows, width), BF16),
            pltpu.VMEM((1, width), F32),
            pltpu.VMEM((n, 1, width), F32),
            pltpu.VMEM((rows, features), BF16),
            pltpu.VMEM(w_query.shape, BF16),
            pltpu.VMEM(w_key.shape, BF16),
            pltpu.VMEM(w_value.shape, BF16),
            pltpu.VMEM(w_out.shape, BF16),
            pltpu.VMEM((rows, heads * DH), F32),
            pltpu.VMEM((own, rows), F32),
            pltpu.VMEM((own, rows), F32),
            pltpu.VMEM((stack, DH), BF16),
            pltpu.VMEM((members, own, rows), BF16),
            pltpu.VMEM((members, own, rows), BF16),
            pltpu.VMEM((n, positions, DH), BF16),
            pltpu.VMEM((n, positions, DH), BF16),
            pltpu.VMEM((n, stack, positions), F32),
            pltpu.VMEM((stack, 128), F32),
            pltpu.VMEM((stack, 128), F32),
            pltpu.VMEM((stack, DH), F32),
            pltpu.VMEM((rows, heads * DH), BF16),
            pltpu.VMEM((chips,) + block, F32),
            pltpu.VMEM((chips,) + block, BF16),
            pltpu.VMEM((chips,) + block, BF16),
            pltpu.VMEM((nz, ny) + block, BF16),
            pltpu.VMEM((nz, ny) + block, BF16),
            pltpu.VMEM((nz,) + block, BF16),
            pltpu.VMEM((nz,) + block, BF16),
            dma((8,)),
            dma((n,)), dma((n,)),
            dma((nz, CHUNKS)), dma((nz, CHUNKS)), dma((nz, ny, CHUNKS)), dma((chips, CHUNKS)),
            dma((n, CHUNKS)),
            dma((chips,)), dma((chips,)), dma((n,)),
            dma((chips,)), dma((chips,)), dma((n,)),
            dma((2, members)), dma((2, members)),
            dma((chips,)), dma((chips,)),
            dma((nz, ny, CUTS)), dma((nz, ny, CUTS)),
            dma((nz, CUTS)), dma((nz, CUTS)),
        ],
        compiler_params=pltpu.CompilerParams(
            collective_id=0, has_side_effects=True, vmem_limit_bytes=60 * 2**20
        ),
    )(tokens, gain, w_query, w_key, w_value, w_out, cache)


def solution(mesh):
    n = mesh.shape["seq"]
    ny = max(1, 4 // mesh.shape["group"])
    return jax.shard_map(
        functools.partial(body, n, ny),
        mesh=mesh,
        in_specs=(
            P("group", "seq"),
            P("seq"),
            P("seq", None),
            P("seq", None),
            P("seq", None),
            P("seq", None),
            P(None, ("group", "seq"), None),
        ),
        out_specs=P("group", "seq"),
        check_vma=False,
    )
```

```python
import functools
import math

import jax
import jax.numpy as jnp
from jax import lax
from jax.experimental import pallas as pl
from jax.experimental.pallas import tpu as pltpu
from jax.sharding import PartitionSpec as P

H = 64
KV = 8
DH = 128
CHUNKS = 2
CUTS = 2
NT = (((1,), (1,)), ((), ()))
MESH = pl.DeviceIdType.MESH
F32 = jnp.float32
BF16 = jnp.bfloat16


def kernel(
    n, ny, tokens, gain_in, w_query, w_key, w_value, w_out, cache, out,
    tok, my_gain, gains, normed, wq, wk, wv, wo, q_acc, k_acc, v_acc, q_rows, k_own, v_own,
    k_buf, v_buf, scores, top, low, numer, att, acc, s1_out, s1_in, s2_out, s2_in, s3_out, s3_in,
    local_sem, gain_send, gain_recv, tok_up, tok_down, tok_send_y, tok_send_c, tok_recv,
    k_send, k_send_c, k_recv, v_send, v_send_c, v_recv, own_send, own_recv,
    s1_send, s1_recv, s2_send, s2_recv, s3_send, s3_recv,
):
    chips = n // 2
    nz = chips // ny
    me = lax.axis_index("seq")
    c = lax.rem(me, 2)
    chip = me // 2
    y = lax.rem(chip, ny)
    z = chip // ny
    partner = chip * 2 + 1 - c
    rows, width = tokens.shape
    heads = H // n
    members = n // KV
    kv_head = me // members
    member = lax.rem(me, members)
    positions = cache.shape[1]
    lanes = [slice(k * 128, (k + 1) * 128) for k in range(positions // 128)]
    scale = 1.0 / math.sqrt(DH)

    def seq_of(z_, y_, c_):
        return (z_ * ny + y_) * 2 + c_

    def other_z(d):
        return lax.rem(z + d, nz)

    def other_y(d):
        return lax.rem(y + d, ny)

    def remote(src, dst, send, recv, to):
        return pltpu.make_async_remote_copy(
            src_ref=src, dst_ref=dst, send_sem=send, recv_sem=recv,
            device_id={"seq": to}, device_id_type=MESH,
        )

    def each(start, stop, step):
        lax.fori_loop(start, stop, lambda i, carry: (step(i), carry)[1], 0)

    weights_in = [
        pltpu.make_async_copy(src, dst, local_sem.at[i])
        for i, (src, dst) in enumerate(
            [(w_query, wq), (w_key, wk), (w_value, wv), (w_out, wo)]
        )
    ]
    own_tok = pltpu.make_async_copy(tokens, tok.at[me], local_sem.at[4])
    gain = my_gain

    def own_cols(to_kv):
        return pl.ds(pl.multiple_of(to_kv * DH, DH), DH)

    own_k = pltpu.make_async_copy(
        cache.at[0, :, own_cols(kv_head)], k_buf.at[me], local_sem.at[6]
    )
    own_v = pltpu.make_async_copy(
        cache.at[1, :, own_cols(kv_head)], v_buf.at[me], local_sem.at[7]
    )

    barrier = pltpu.get_barrier_semaphore()

    def greet(to):
        pl.semaphore_signal(barrier, inc=1, device_id={"seq": to}, device_id_type=MESH)

    @pl.when(z >= 1)
    def _():
        greet(seq_of(z - 1, y, c))

    @pl.when(z + 1 < nz)
    def _():
        greet(seq_of(z + 1, y, c))

    for d_y in range(1, ny):
        greet(seq_of(z, other_y(d_y), c))
    greet(partner)
    own_tok.start()
    for copy in weights_in:
        copy.start()
    my_gain[...] = gain_in[...].astype(F32).reshape(1, width)
    gains[me] = my_gain[...]
    pl.semaphore_wait(
        barrier, ny + jnp.where(z >= 1, 1, 0) + jnp.where(z + 1 < nz, 1, 0))

    chunks = tok_recv.shape[1]
    deep = rows // chunks

    def piece_of(slot, k):
        return tok.at[slot, pl.ds(pl.multiple_of(k * deep, deep), deep), :]

    def tok_z(slot, k, d, up):
        ends = tok_up if up else tok_down
        to = jnp.clip(z + (1 if up else -1), 0, nz - 1)
        return remote(piece_of(slot, k), piece_of(slot, k), ends.at[d, k],
                      tok_recv.at[slot, k], seq_of(to, y, c))

    def tok_y(slot, k, d_z, d_y):
        return remote(piece_of(slot, k), piece_of(slot, k), tok_send_y.at[d_z, d_y, k],
                      tok_recv.at[slot, k], seq_of(z, other_y(d_y), c))

    def tok_c(slot, k):
        return remote(piece_of(slot, k), piece_of(slot, k), tok_send_c.at[slot // 2, k],
                      tok_recv.at[slot, k], partner)

    def tok_wait(slot, k):
        remote(piece_of(slot, k), piece_of(slot, k), tok_send_c.at[0, k], tok_recv.at[slot, k],
               partner).wait_recv()

    own_tok.wait()

    def send_own(k):
        @pl.when(z + 1 < nz)
        def _():
            tok_z(me, k, 0, True).start()

        @pl.when(z >= 1)
        def _():
            tok_z(me, k, 0, False).start()

        for d_y in range(1, ny):
            tok_y(me, k, z, d_y).start()
        tok_c(me, k).start()

    each(0, chunks, send_own)

    def gain_copy(i):
        return remote(gain, gains.at[me], gain_send.at[i], gain_recv.at[me],
                      lax.rem(chip + i, chips) * 2 + c)

    def gain_pair(i):
        slot = lax.rem(chip + i, chips) * 2 + c
        return remote(gains.at[slot], gains.at[slot], gain_send.at[chips + i],
                      gain_recv.at[slot], partner)

    def kv_copy(half, buf, send, recv, i):
        other = lax.rem(chip + i, chips)
        to = other * 2 + c
        return remote(cache.at[half, :, own_cols(to // members)], buf.at[me], send.at[i],
                      recv.at[me], to)

    def kv_pair(src, buf, send, recv, slot):
        return remote(src, buf.at[slot], send.at[slot // 2], recv.at[slot], partner)

    def kv_wait(buf, send, recv, slot):
        remote(buf.at[slot], buf.at[slot], send.at[0], recv.at[slot], partner).wait_recv()

    def k_copy(i):
        return kv_copy(0, k_buf, k_send, k_recv, i)

    def v_copy(i):
        return kv_copy(1, v_buf, v_send, v_recv, i)


    def forward_z(i):
        d = 1 + i // chunks
        k = lax.rem(i, chunks)

        def pass_on(slot, up):
            tok_wait(slot, k)

            @pl.when((z + 1 < nz) if up else (z >= 1))
            def _():
                tok_z(slot, k, d, up).start()

            for d_y in range(1, ny):
                tok_y(slot, k, slot // (2 * ny), d_y).start()
            tok_c(slot, k).start()

        @pl.when(z - d >= 0)
        def _():
            pass_on(seq_of(z - d, y, c), True)

        @pl.when(z + d < nz)
        def _():
            pass_on(seq_of(z + d, y, c), False)

    each(0, (nz - 1) * chunks, forward_z)
    each(1, chips, lambda i: gain_copy(i).start())
    gain_pair(0).start()
    each(1, chips, lambda i: k_copy(i).start())
    k_own_src = cache.at[0, :, own_cols(kv_head)]
    v_own_src = cache.at[1, :, own_cols(kv_head)]
    kv_pair(k_own_src, k_buf, k_send_c, k_recv, me).start()
    own_k.start()


    def spread(i):
        reach = jnp.minimum(z, nz - 1 - z)
        side = jnp.where(lax.rem(i, 2) == 1, z - (i + 1) // 2, z + i // 2)
        return jnp.where(i <= 2 * reach, side, jnp.where(z < nz - 1 - z, i, nz - 1 - i))

    for d_y in range(1, ny):
        def forward_y(i, d_y=d_y):
            there = seq_of(spread(i // chunks), other_y(d_y), c)
            k = lax.rem(i, chunks)
            tok_wait(there, k)
            tok_c(there, k).start()
        each(0, nz * chunks, forward_y)

    each(1, chips, lambda i: v_copy(i).start())

    def gain_wait(slot):
        remote(gain, gains.at[slot], gain_send.at[0], gain_recv.at[slot], partner).wait_recv()

    def gain_step(i):
        gain_wait(lax.rem(chip + i, chips) * 2 + c)
        gain_pair(i).start()

    each(1, chips, gain_step)
    kv_pair(v_own_src, v_buf, v_send_c, v_recv, me).start()
    own_v.start()

    each(0, chips * chunks, lambda i: tok_wait((i // chunks) * 2 + 1 - c, lax.rem(i, chunks)))

    parts = width // 128

    def square_step(b, total):
        x = tok[b].astype(F32)
        for k in range(parts):
            piece = x[:, k * 128:(k + 1) * 128]
            total = total + piece * piece
        return total

    total = lax.fori_loop(0, n, square_step, jnp.zeros((rows, 128), F32))
    each(0, chips, lambda i: gain_wait(i * 2 + 1 - c))
    mean = jnp.sum(total, axis=1, keepdims=True) * (1.0 / (n * width))
    inverse = jnp.broadcast_to(lax.rsqrt(mean + 1e-05), (rows, 128))

    def norm_step(b):
        for k in range(parts):
            x = tok[b, :, k * 128:(k + 1) * 128].astype(F32)
            g = gains[b, :, k * 128:(k + 1) * 128].astype(F32)
            normed[:, pl.ds(pl.multiple_of(b * width + k * 128, 128), 128)] = (
                x * inverse * g).astype(BF16)

    each(0, n, norm_step)

    for copy in weights_in[:3]:
        copy.wait()
    q_acc[...] = jnp.zeros_like(q_acc)
    k_acc[...] = jnp.zeros_like(k_acc)
    v_acc[...] = jnp.zeros_like(v_acc)
    depth = 1024

    def project(i):
        cols = pl.ds(pl.multiple_of(i * depth, depth), depth)
        x = normed[:, cols]
        k_acc[...] += lax.dot_general(wk[:, cols], x, NT, preferred_element_type=F32)
        v_acc[...] += lax.dot_general(wv[:, cols], x, NT, preferred_element_type=F32)
        q_acc[...] += lax.dot_general(x, wq[:, cols], NT, preferred_element_type=F32)

    each(0, normed.shape[1] // depth, project)
    k_own[member] = k_acc[...].astype(BF16)
    v_own[member] = v_acc[...].astype(BF16)

    def own_copy(which, buf, i):
        return remote(buf.at[member], buf.at[member], own_send.at[which, i],
                      own_recv.at[which, member], kv_head * members + lax.rem(member + i, members))

    def own_wait(which, buf, i):
        slot = lax.rem(member + i, members)
        remote(buf.at[slot], buf.at[slot], own_send.at[which, 0], own_recv.at[which, slot],
               partner).wait_recv()

    for i in range(1, members):
        own_copy(0, k_own, i).start()
        own_copy(1, v_own, i).start()

    for h in range(heads):
        q_rows[h * rows:(h + 1) * rows, :] = q_acc[:, h * DH:(h + 1) * DH].astype(BF16)

    top[...] = jnp.full_like(top, -jnp.inf)

    def score_block(slot):
        keys = k_buf[slot]
        for h in range(heads):
            here = slice(h * rows, (h + 1) * rows)
            s = lax.dot_general(q_rows[here, :], keys, NT, preferred_element_type=F32) * scale
            scores[slot, here, :] = s
            best = top[here, :]
            for part in lanes:
                best = jnp.maximum(best, s[:, part])
            top[here, :] = best

    own_k.wait()
    score_block(me)

    def k_mine(i):
        slot = lax.rem(chip + chips - i, chips) * 2 + c
        kv_wait(k_buf, k_send_c, k_recv, slot)
        kv_pair(k_buf.at[slot], k_buf, k_send_c, k_recv, slot).start()
        score_block(slot)

    each(1, chips, k_mine)

    def k_theirs(i):
        slot = lax.rem(chip + chips - i, chips) * 2 + 1 - c
        kv_wait(k_buf, k_send_c, k_recv, slot)
        score_block(slot)

    each(0, chips, k_theirs)

    for i in range(1, members):
        own_wait(0, k_own, i)
        own_wait(1, v_own, i)
    key_rows = k_own[...].astype(F32).reshape(DH, rows).T
    own_scores = []
    for h in range(heads):
        here = slice(h * rows, (h + 1) * rows)
        own = jnp.sum(q_rows[here, :].astype(F32) * key_rows, axis=1, keepdims=True) * scale
        best = jnp.maximum(jnp.max(top[here, :], axis=1, keepdims=True), own)
        top[here, :] = jnp.broadcast_to(best, (rows, 128))
        own_scores.append(jnp.exp(own - best))

    low[...] = jnp.zeros_like(low)
    numer[...] = jnp.zeros_like(numer)

    def value_block(slot):
        values = v_buf[slot]
        for h in range(heads):
            here = slice(h * rows, (h + 1) * rows)
            best = top[here, :]
            pieces = [jnp.exp(scores[slot, here, part] - best) for part in lanes]
            low[here, :] += functools.reduce(jnp.add, pieces)
            weights = jnp.concatenate([piece.astype(BF16) for piece in pieces], axis=1)
            numer[here, :] += jnp.dot(weights, values, preferred_element_type=F32)

    own_v.wait()
    value_block(me)

    def v_mine(i):
        slot = lax.rem(chip + chips - i, chips) * 2 + c
        kv_wait(v_buf, v_send_c, v_recv, slot)
        kv_pair(v_buf.at[slot], v_buf, v_send_c, v_recv, slot).start()
        value_block(slot)

    each(1, chips, v_mine)

    def v_theirs(i):
        slot = lax.rem(chip + chips - i, chips) * 2 + 1 - c
        kv_wait(v_buf, v_send_c, v_recv, slot)
        value_block(slot)

    each(0, chips, v_theirs)

    value_rows = v_own[...].astype(F32).reshape(DH, rows).T
    for h in range(heads):
        here = slice(h * rows, (h + 1) * rows)
        own_weight = own_scores[h]
        denom = jnp.sum(low[here, :], axis=1, keepdims=True) + own_weight
        total = numer[here, :] + own_weight.astype(BF16).astype(F32) * value_rows
        att[:, h * DH:(h + 1) * DH] = (total / denom).astype(BF16)

    weights_in[3].wait()

    def partial_for(to):
        cols = pl.ds(pl.multiple_of(to * width, width), width)
        return jnp.dot(att[...], wo[:, cols], preferred_element_type=F32)

    def s1_copy(target):
        return remote(s1_out.at[target], s1_in.at[target], s1_send.at[target],
                      s1_recv.at[target], partner)

    cuts = s2_send.shape[2]
    short = rows // cuts
    pieces = [slice(k * short, (k + 1) * short) for k in range(cuts)]

    def s2_copy(d_z, d_y, k):
        return remote(s2_out.at[d_z, d_y, pieces[k]], s2_in.at[d_z, d_y, pieces[k]],
                      s2_send.at[d_z, d_y, k], s2_recv.at[d_z, d_y, k], seq_of(z, other_y(d_y), c))

    def s3_copy(d, k):
        return remote(s3_out.at[d, pieces[k]], s3_in.at[d, pieces[k]], s3_send.at[d, k],
                      s3_recv.at[d, k], seq_of(other_z(d), y, c))

    def distance(i):
        down = nz - 1 - i
        down = jnp.where(down <= z, down - 1, down)
        up = jnp.where(i >= z, i + 1, i)
        there = jnp.where(z < nz - 1 - z, down, up)
        return lax.rem(jnp.where(i == nz - 1, z, there) - z + nz, nz)

    def give(i, d_y):
        target = other_z(distance(i)) * ny + other_y(d_y)
        s1_out[target] = partial_for(target * 2 + 1 - c).astype(BF16)
        s1_copy(target).start()

    def keep(i, d_y):
        target = other_z(distance(i)) * ny + other_y(d_y)
        acc[target] = partial_for(target * 2 + c)

    def step_two(i, d_y):
        d = distance(i)
        keep(i, d_y)
        target = other_z(d) * ny + other_y(d_y)
        s1_copy(target).wait_recv()
        for k, here in enumerate(pieces):
            s2_out[d, d_y, here, :] = (
                acc[target, here, :] + s1_in[target, here, :].astype(F32)).astype(BF16)
            s2_copy(d, d_y, k).start()

    def column_sum(d, k):
        here = pieces[k]
        target = other_z(d) * ny + y
        total = acc[target, here, :] + s1_in[target, here, :].astype(F32)
        for d_y in range(1, ny):
            s2_copy(d, d_y, k).wait_recv()
            total = total + s2_in[d, d_y, here, :].astype(F32)
        return total

    def step_three(i):
        d = distance(i)
        s1_copy(other_z(d) * ny + y).wait_recv()
        for k, here in enumerate(pieces):
            s3_out[d, here, :] = column_sum(d, k).astype(BF16)
            s3_copy(d, k).start()

    for d_y in range(1, ny):
        each(0, nz, functools.partial(give, d_y=d_y))
        each(0, nz, functools.partial(step_two, d_y=d_y))
    each(0, nz, functools.partial(give, d_y=0))
    each(0, nz, functools.partial(keep, d_y=0))
    each(0, nz - 1, step_three)
    s1_copy(chip).wait_recv()
    for k, here in enumerate(pieces):
        acc[chip, here, :] = column_sum(0, k)

    def last(d):
        for k, here in enumerate(pieces):
            s3_copy(d, k).wait_recv()
            acc[chip, here, :] += s3_in[d, here, :].astype(F32)

    each(1, nz, last)
    out[...] = acc[chip].astype(out.dtype)

    def tok_sent(i):
        d = i // chunks
        k = lax.rem(i, chunks)

        @pl.when((z - d >= 0) & (z + 1 < nz))
        def _():
            tok_z(seq_of(z - d, y, c), k, d, True).wait_send()

        @pl.when((z + d < nz) & (z >= 1))
        def _():
            tok_z(seq_of(z + d, y, c), k, d, False).wait_send()

        for d_y in range(1, ny):
            tok_y(me, k, d, d_y).wait_send()

    each(0, nz * chunks, tok_sent)
    each(0, chips * chunks, lambda i: tok_c(
        (i // chunks) * 2 + c, lax.rem(i, chunks)).wait_send())
    each(1, chips, lambda i: gain_copy(i).wait_send())
    each(0, chips, lambda i: gain_pair(i).wait_send())
    each(1, chips, lambda i: k_copy(i).wait_send())
    each(1, chips, lambda i: v_copy(i).wait_send())

    def core_sent(i):
        slot = i * 2 + c
        kv_pair(k_buf.at[slot], k_buf, k_send_c, k_recv, slot).wait_send()
        kv_pair(v_buf.at[slot], v_buf, v_send_c, v_recv, slot).wait_send()
        s1_copy(i).wait_send()

    each(0, chips, core_sent)
    for i in range(1, members):
        own_copy(0, k_own, i).wait_send()
        own_copy(1, v_own, i).wait_send()
    for d_y in range(1, ny):
        for k in range(cuts):
            each(0, nz, lambda d, d_y=d_y, k=k: s2_copy(d, d_y, k).wait_send())
    for k in range(cuts):
        each(1, nz, lambda d, k=k: s3_copy(d, k).wait_send())


def body(n, ny, tokens, gain, w_query, w_key, w_value, w_out, cache):
    rows, width = tokens.shape
    features = w_query.shape[1]
    heads = H // n
    chips = n // 2
    nz = chips // ny
    members = n // KV
    own = w_key.shape[0]
    positions = cache.shape[1]
    stack = heads * rows
    dma = pltpu.SemaphoreType.DMA
    hbm = pl.BlockSpec(memory_space=pl.ANY)
    vmem = pl.BlockSpec(memory_space=pltpu.VMEM)
    block = (rows, width)
    return pl.pallas_call(
        functools.partial(kernel, n, ny),
        out_shape=jax.ShapeDtypeStruct((rows, width), BF16),
        in_specs=[vmem, vmem, hbm, hbm, hbm, hbm, hbm],
        out_specs=vmem,
        scratch_shapes=[
            pltpu.VMEM((n, rows, width), BF16),
            pltpu.VMEM((1, width), F32),
            pltpu.VMEM((n, 1, width), F32),
            pltpu.VMEM((rows, features), BF16),
            pltpu.VMEM(w_query.shape, BF16),
            pltpu.VMEM(w_key.shape, BF16),
            pltpu.VMEM(w_value.shape, BF16),
            pltpu.VMEM(w_out.shape, BF16),
            pltpu.VMEM((rows, heads * DH), F32),
            pltpu.VMEM((own, rows), F32),
            pltpu.VMEM((own, rows), F32),
            pltpu.VMEM((stack, DH), BF16),
            pltpu.VMEM((members, own, rows), BF16),
            pltpu.VMEM((members, own, rows), BF16),
            pltpu.VMEM((n, positions, DH), BF16),
            pltpu.VMEM((n, positions, DH), BF16),
            pltpu.VMEM((n, stack, positions), F32),
            pltpu.VMEM((stack, 128), F32),
            pltpu.VMEM((stack, 128), F32),
            pltpu.VMEM((stack, DH), F32),
            pltpu.VMEM((rows, heads * DH), BF16),
            pltpu.VMEM((chips,) + block, F32),
            pltpu.VMEM((chips,) + block, BF16),
            pltpu.VMEM((chips,) + block, BF16),
            pltpu.VMEM((nz, ny) + block, BF16),
            pltpu.VMEM((nz, ny) + block, BF16),
            pltpu.VMEM((nz,) + block, BF16),
            pltpu.VMEM((nz,) + block, BF16),
            dma((8,)),
            dma((n,)), dma((n,)),
            dma((nz, CHUNKS)), dma((nz, CHUNKS)), dma((nz, ny, CHUNKS)), dma((chips, CHUNKS)),
            dma((n, CHUNKS)),
            dma((chips,)), dma((chips,)), dma((n,)),
            dma((chips,)), dma((chips,)), dma((n,)),
            dma((2, members)), dma((2, members)),
            dma((chips,)), dma((chips,)),
            dma((nz, ny, CUTS)), dma((nz, ny, CUTS)),
            dma((nz, CUTS)), dma((nz, CUTS)),
        ],
        compiler_params=pltpu.CompilerParams(
            collective_id=0, has_side_effects=True, vmem_limit_bytes=60 * 2**20
        ),
    )(tokens, gain, w_query, w_key, w_value, w_out, cache)


def solution(mesh):
    n = mesh.shape["seq"]
    ny = max(1, 4 // mesh.shape["group"])
    return jax.shard_map(
        functools.partial(body, n, ny),
        mesh=mesh,
        in_specs=(
            P("group", "seq"),
            P("seq"),
            P("seq", None),
            P("seq", None),
            P("seq", None),
            P("seq", None),
            P(None, ("group", "seq"), None),
        ),
        out_specs=P("group", "seq"),
        check_vma=False,
    )
```

```python
import functools
import math

import jax
import jax.numpy as jnp
from jax import lax
from jax.experimental import pallas as pl
from jax.experimental.pallas import tpu as pltpu
from jax.sharding import PartitionSpec as P

H = 64
KV = 8
DH = 128
CHUNKS = 2
CUTS = 2
OWN = 2
LEAD = 2
V_AT = 2
NT = (((1,), (1,)), ((), ()))
MESH = pl.DeviceIdType.MESH
F32 = jnp.float32
BF16 = jnp.bfloat16


def kernel(
    n, ny, tokens, gain_in, w_query, w_key, w_value, w_out, cache, out,
    tok, my_gain, gains, normed, wq, wk, wv, wo, q_acc, k_acc, v_acc, q_rows, k_own, v_own,
    k_buf, v_buf, scores, top, low, numer, att, acc, s1_out, s1_in, s2_out, s2_in, s3_out, s3_in,
    local_sem, gain_send, gain_recv, tok_up, tok_down, tok_send_y, tok_send_c, tok_recv,
    k_send, k_send_c, k_recv, v_send, v_send_c, v_recv, own_send, own_recv,
    s1_send, s1_recv, s2_send, s2_recv, s3_send, s3_recv,
):
    chips = n // 2
    nz = chips // ny
    me = lax.axis_index("seq")
    c = lax.rem(me, 2)
    chip = me // 2
    y = lax.rem(chip, ny)
    z = chip // ny
    partner = chip * 2 + 1 - c
    rows, width = tokens.shape
    heads = H // n
    members = n // KV
    kv_head = me // members
    member = lax.rem(me, members)
    positions = cache.shape[1]
    lanes = [slice(k * 128, (k + 1) * 128) for k in range(positions // 128)]
    scale = 1.0 / math.sqrt(DH)

    def seq_of(z_, y_, c_):
        return (z_ * ny + y_) * 2 + c_

    def other_z(d):
        return lax.rem(z + d, nz)

    def other_y(d):
        return lax.rem(y + d, ny)

    def remote(src, dst, send, recv, to):
        return pltpu.make_async_remote_copy(
            src_ref=src, dst_ref=dst, send_sem=send, recv_sem=recv,
            device_id={"seq": to}, device_id_type=MESH,
        )

    def each(start, stop, step):
        lax.fori_loop(start, stop, lambda i, carry: (step(i), carry)[1], 0)

    weights_in = [
        pltpu.make_async_copy(src, dst, local_sem.at[i])
        for i, (src, dst) in enumerate(
            [(w_query, wq), (w_key, wk), (w_value, wv), (w_out, wo)]
        )
    ]
    own_tok = pltpu.make_async_copy(tokens, tok.at[me], local_sem.at[4])
    gain = my_gain

    def own_cols(to_kv):
        return pl.ds(pl.multiple_of(to_kv * DH, DH), DH)

    own_k = pltpu.make_async_copy(
        cache.at[0, :, own_cols(kv_head)], k_buf.at[me], local_sem.at[6]
    )
    own_v = pltpu.make_async_copy(
        cache.at[1, :, own_cols(kv_head)], v_buf.at[me], local_sem.at[7]
    )

    barrier = pltpu.get_barrier_semaphore()

    def greet(to):
        pl.semaphore_signal(barrier, inc=1, device_id={"seq": to}, device_id_type=MESH)

    @pl.when(z >= 1)
    def _():
        greet(seq_of(z - 1, y, c))

    @pl.when(z + 1 < nz)
    def _():
        greet(seq_of(z + 1, y, c))

    for d_y in range(1, ny):
        greet(seq_of(z, other_y(d_y), c))
    greet(partner)
    own_tok.start()
    for copy in weights_in:
        copy.start()
    my_gain[...] = gain_in[...].astype(F32).reshape(1, width)
    gains[me] = my_gain[...]
    pl.semaphore_wait(
        barrier, ny + jnp.where(z >= 1, 1, 0) + jnp.where(z + 1 < nz, 1, 0))

    chunks = tok_recv.shape[1]
    deep = rows // chunks

    def piece_of(slot, k):
        return tok.at[slot, pl.ds(pl.multiple_of(k * deep, deep), deep), :]

    def tok_z(slot, k, d, up):
        ends = tok_up if up else tok_down
        to = jnp.clip(z + (1 if up else -1), 0, nz - 1)
        return remote(piece_of(slot, k), piece_of(slot, k), ends.at[d, k],
                      tok_recv.at[slot, k], seq_of(to, y, c))

    def tok_y(slot, k, d_z, d_y):
        return remote(piece_of(slot, k), piece_of(slot, k), tok_send_y.at[d_z, d_y, k],
                      tok_recv.at[slot, k], seq_of(z, other_y(d_y), c))

    def tok_c(slot, k):
        return remote(piece_of(slot, k), piece_of(slot, k), tok_send_c.at[slot // 2, k],
                      tok_recv.at[slot, k], partner)

    def tok_wait(slot, k):
        remote(piece_of(slot, k), piece_of(slot, k), tok_send_c.at[0, k], tok_recv.at[slot, k],
               partner).wait_recv()

    own_tok.wait()

    def send_own(k):
        if OWN == 1:
            for d_y in range(1, ny):
                tok_y(me, k, z, d_y).start()

        lower = z < nz - 1 - z

        @pl.when((z + 1 < nz) & lower)
        def _():
            tok_z(me, k, 0, True).start()

        @pl.when(z >= 1)
        def _():
            tok_z(me, k, 0, False).start()

        @pl.when((z + 1 < nz) & jnp.logical_not(lower))
        def _():
            tok_z(me, k, 0, True).start()

        if OWN == 2:
            for d_y in range(1, ny):
                tok_y(me, k, z, d_y).start()
        tok_c(me, k).start()

    each(0, chunks, send_own)

    def gain_copy(i):
        return remote(gain, gains.at[me], gain_send.at[i], gain_recv.at[me],
                      lax.rem(chip + i, chips) * 2 + c)

    def gain_pair(i):
        slot = lax.rem(chip + i, chips) * 2 + c
        return remote(gains.at[slot], gains.at[slot], gain_send.at[chips + i],
                      gain_recv.at[slot], partner)

    def kv_copy(half, buf, send, recv, i):
        other = lax.rem(chip + i, chips)
        to = other * 2 + c
        return remote(cache.at[half, :, own_cols(to // members)], buf.at[me], send.at[i],
                      recv.at[me], to)

    def kv_pair(src, buf, send, recv, slot):
        return remote(src, buf.at[slot], send.at[slot // 2], recv.at[slot], partner)

    def kv_wait(buf, send, recv, slot):
        remote(buf.at[slot], buf.at[slot], send.at[0], recv.at[slot], partner).wait_recv()

    def k_copy(i):
        return kv_copy(0, k_buf, k_send, k_recv, i)

    def v_copy(i):
        return kv_copy(1, v_buf, v_send, v_recv, i)


    def forward_z(i):
        d = 1 + i // chunks
        k = lax.rem(i, chunks)

        def pass_on(slot, up):
            tok_wait(slot, k)

            @pl.when((z + 1 < nz) if up else (z >= 1))
            def _():
                tok_z(slot, k, d, up).start()

            for d_y in range(1, ny):
                tok_y(slot, k, slot // (2 * ny), d_y).start()
            tok_c(slot, k).start()

        @pl.when(z - d >= 0)
        def _():
            pass_on(seq_of(z - d, y, c), True)

        @pl.when(z + d < nz)
        def _():
            pass_on(seq_of(z + d, y, c), False)

    each(0, (nz - 1) * chunks, forward_z)
    each(1, chips, lambda i: gain_copy(i).start())
    gain_pair(0).start()
    each(1, chips, lambda i: k_copy(i).start())
    k_own_src = cache.at[0, :, own_cols(kv_head)]
    v_own_src = cache.at[1, :, own_cols(kv_head)]
    kv_pair(k_own_src, k_buf, k_send_c, k_recv, me).start()
    own_k.start()


    def spread(i):
        reach = jnp.minimum(z, nz - 1 - z)
        side = jnp.where(lax.rem(i, 2) == 1, z - (i + 1) // 2, z + i // 2)
        return jnp.where(i <= 2 * reach, side, jnp.where(z < nz - 1 - z, i, nz - 1 - i))

    for d_y in range(1, ny):
        def forward_y(i, d_y=d_y):
            there = seq_of(spread(i // chunks), other_y(d_y), c)
            k = lax.rem(i, chunks)
            tok_wait(there, k)
            tok_c(there, k).start()
        each(0, nz * chunks, forward_y)

    if V_AT == 2:
        each(1, chips, lambda i: v_copy(i).start())

    def gain_wait(slot):
        remote(gain, gains.at[slot], gain_send.at[0], gain_recv.at[slot], partner).wait_recv()

    def gain_step(i):
        gain_wait(lax.rem(chip + i, chips) * 2 + c)
        gain_pair(i).start()

    each(1, chips, gain_step)
    kv_pair(v_own_src, v_buf, v_send_c, v_recv, me).start()
    own_v.start()

    if V_AT == 3:
        each(1, chips, lambda i: v_copy(i).start())
    each(0, chips * chunks, lambda i: tok_wait((i // chunks) * 2 + 1 - c, lax.rem(i, chunks)))

    parts = width // 128

    def square_step(b, total):
        x = tok[b].astype(F32)
        for k in range(parts):
            piece = x[:, k * 128:(k + 1) * 128]
            total = total + piece * piece
        return total

    total = lax.fori_loop(0, n, square_step, jnp.zeros((rows, 128), F32))
    each(0, chips, lambda i: gain_wait(i * 2 + 1 - c))
    mean = jnp.sum(total, axis=1, keepdims=True) * (1.0 / (n * width))
    inverse = jnp.broadcast_to(lax.rsqrt(mean + 1e-05), (rows, 128))

    def norm_step(b):
        for k in range(parts):
            x = tok[b, :, k * 128:(k + 1) * 128].astype(F32)
            g = gains[b, :, k * 128:(k + 1) * 128].astype(F32)
            normed[:, pl.ds(pl.multiple_of(b * width + k * 128, 128), 128)] = (
                x * inverse * g).astype(BF16)

    each(0, n, norm_step)

    for copy in weights_in[:3]:
        copy.wait()
    q_acc[...] = jnp.zeros_like(q_acc)
    k_acc[...] = jnp.zeros_like(k_acc)
    v_acc[...] = jnp.zeros_like(v_acc)
    depth = 1024

    def project(i):
        cols = pl.ds(pl.multiple_of(i * depth, depth), depth)
        x = normed[:, cols]
        k_acc[...] += lax.dot_general(wk[:, cols], x, NT, preferred_element_type=F32)
        v_acc[...] += lax.dot_general(wv[:, cols], x, NT, preferred_element_type=F32)
        q_acc[...] += lax.dot_general(x, wq[:, cols], NT, preferred_element_type=F32)

    each(0, normed.shape[1] // depth, project)
    k_own[member] = k_acc[...].astype(BF16)
    v_own[member] = v_acc[...].astype(BF16)

    def own_copy(which, buf, i):
        return remote(buf.at[member], buf.at[member], own_send.at[which, i],
                      own_recv.at[which, member], kv_head * members + lax.rem(member + i, members))

    def own_wait(which, buf, i):
        slot = lax.rem(member + i, members)
        remote(buf.at[slot], buf.at[slot], own_send.at[which, 0], own_recv.at[which, slot],
               partner).wait_recv()

    for i in range(1, members):
        own_copy(0, k_own, i).start()
        own_copy(1, v_own, i).start()

    for h in range(heads):
        q_rows[h * rows:(h + 1) * rows, :] = q_acc[:, h * DH:(h + 1) * DH].astype(BF16)

    top[...] = jnp.full_like(top, -jnp.inf)

    def score_block(slot):
        keys = k_buf[slot]
        for h in range(heads):
            here = slice(h * rows, (h + 1) * rows)
            s = lax.dot_general(q_rows[here, :], keys, NT, preferred_element_type=F32) * scale
            scores[slot, here, :] = s
            best = top[here, :]
            for part in lanes:
                best = jnp.maximum(best, s[:, part])
            top[here, :] = best

    own_k.wait()
    score_block(me)

    def k_mine(i):
        slot = lax.rem(chip + chips - i, chips) * 2 + c
        kv_wait(k_buf, k_send_c, k_recv, slot)
        kv_pair(k_buf.at[slot], k_buf, k_send_c, k_recv, slot).start()
        score_block(slot)

    each(1, chips, k_mine)

    def k_theirs(i):
        slot = lax.rem(chip + chips - i, chips) * 2 + 1 - c
        kv_wait(k_buf, k_send_c, k_recv, slot)
        score_block(slot)

    each(0, chips, k_theirs)

    for i in range(1, members):
        own_wait(0, k_own, i)
        own_wait(1, v_own, i)
    key_rows = k_own[...].astype(F32).reshape(DH, rows).T
    own_scores = []
    for h in range(heads):
        here = slice(h * rows, (h + 1) * rows)
        own = jnp.sum(q_rows[here, :].astype(F32) * key_rows, axis=1, keepdims=True) * scale
        best = jnp.maximum(jnp.max(top[here, :], axis=1, keepdims=True), own)
        top[here, :] = jnp.broadcast_to(best, (rows, 128))
        own_scores.append(jnp.exp(own - best))

    low[...] = jnp.zeros_like(low)
    numer[...] = jnp.zeros_like(numer)

    def value_block(slot):
        values = v_buf[slot]
        for h in range(heads):
            here = slice(h * rows, (h + 1) * rows)
            best = top[here, :]
            pieces = [jnp.exp(scores[slot, here, part] - best) for part in lanes]
            low[here, :] += functools.reduce(jnp.add, pieces)
            weights = jnp.concatenate([piece.astype(BF16) for piece in pieces], axis=1)
            numer[here, :] += jnp.dot(weights, values, preferred_element_type=F32)

    own_v.wait()
    value_block(me)

    def v_mine(i):
        slot = lax.rem(chip + chips - i, chips) * 2 + c
        kv_wait(v_buf, v_send_c, v_recv, slot)
        kv_pair(v_buf.at[slot], v_buf, v_send_c, v_recv, slot).start()
        value_block(slot)

    each(1, chips, v_mine)

    def v_theirs(i):
        slot = lax.rem(chip + chips - i, chips) * 2 + 1 - c
        kv_wait(v_buf, v_send_c, v_recv, slot)
        value_block(slot)

    each(0, chips, v_theirs)

    value_rows = v_own[...].astype(F32).reshape(DH, rows).T
    for h in range(heads):
        here = slice(h * rows, (h + 1) * rows)
        own_weight = own_scores[h]
        denom = jnp.sum(low[here, :], axis=1, keepdims=True) + own_weight
        total = numer[here, :] + own_weight.astype(BF16).astype(F32) * value_rows
        att[:, h * DH:(h + 1) * DH] = (total / denom).astype(BF16)

    weights_in[3].wait()

    def partial_for(to):
        cols = pl.ds(pl.multiple_of(to * width, width), width)
        return jnp.dot(att[...], wo[:, cols], preferred_element_type=F32)

    def s1_copy(target):
        return remote(s1_out.at[target], s1_in.at[target], s1_send.at[target],
                      s1_recv.at[target], partner)

    cuts = s2_send.shape[2]
    short = rows // cuts
    pieces = [slice(k * short, (k + 1) * short) for k in range(cuts)]

    def s2_copy(d_z, d_y, k):
        return remote(s2_out.at[d_z, d_y, pieces[k]], s2_in.at[d_z, d_y, pieces[k]],
                      s2_send.at[d_z, d_y, k], s2_recv.at[d_z, d_y, k], seq_of(z, other_y(d_y), c))

    def s3_copy(d, k):
        return remote(s3_out.at[d, pieces[k]], s3_in.at[d, pieces[k]], s3_send.at[d, k],
                      s3_recv.at[d, k], seq_of(other_z(d), y, c))

    def distance(i):
        down = nz - 1 - i
        down = jnp.where(down <= z, down - 1, down)
        up = jnp.where(i >= z, i + 1, i)
        there = jnp.where(z < nz - 1 - z, down, up)
        return lax.rem(jnp.where(i == nz - 1, z, there) - z + nz, nz)

    def give(i, d_y):
        target = other_z(distance(i)) * ny + other_y(d_y)
        s1_out[target] = partial_for(target * 2 + 1 - c).astype(BF16)
        s1_copy(target).start()

    def keep(i, d_y):
        target = other_z(distance(i)) * ny + other_y(d_y)
        acc[target] = partial_for(target * 2 + c)

    def step_two(i, d_y):
        d = distance(i)
        keep(i, d_y)
        target = other_z(d) * ny + other_y(d_y)
        s1_copy(target).wait_recv()
        for k, here in enumerate(pieces):
            s2_out[d, d_y, here, :] = (
                acc[target, here, :] + s1_in[target, here, :].astype(F32)).astype(BF16)
            s2_copy(d, d_y, k).start()

    def column_sum(d, k):
        here = pieces[k]
        target = other_z(d) * ny + y
        total = acc[target, here, :] + s1_in[target, here, :].astype(F32)
        for d_y in range(1, ny):
            s2_copy(d, d_y, k).wait_recv()
            total = total + s2_in[d, d_y, here, :].astype(F32)
        return total

    def step_three(i):
        d = distance(i)
        s1_copy(other_z(d) * ny + y).wait_recv()
        for k, here in enumerate(pieces):
            s3_out[d, here, :] = column_sum(d, k).astype(BF16)
            s3_copy(d, k).start()

    for d_y in range(1, ny):
        if LEAD:
            each(0, LEAD, functools.partial(give, d_y=d_y))
            each(LEAD, nz, lambda i, d_y=d_y: (give(i, d_y), step_two(i - LEAD, d_y)))
            each(nz - LEAD, nz, functools.partial(step_two, d_y=d_y))
        else:
            each(0, nz, functools.partial(give, d_y=d_y))
            each(0, nz, functools.partial(step_two, d_y=d_y))
    each(0, nz, functools.partial(give, d_y=0))
    each(0, nz, functools.partial(keep, d_y=0))
    each(0, nz - 1, step_three)
    s1_copy(chip).wait_recv()
    for k, here in enumerate(pieces):
        acc[chip, here, :] = column_sum(0, k)

    def last(d):
        for k, here in enumerate(pieces):
            s3_copy(d, k).wait_recv()
            acc[chip, here, :] += s3_in[d, here, :].astype(F32)

    each(1, nz, last)
    out[...] = acc[chip].astype(out.dtype)

    def tok_sent(i):
        d = i // chunks
        k = lax.rem(i, chunks)

        @pl.when((z - d >= 0) & (z + 1 < nz))
        def _():
            tok_z(seq_of(z - d, y, c), k, d, True).wait_send()

        @pl.when((z + d < nz) & (z >= 1))
        def _():
            tok_z(seq_of(z + d, y, c), k, d, False).wait_send()

        for d_y in range(1, ny):
            tok_y(me, k, d, d_y).wait_send()

    each(0, nz * chunks, tok_sent)
    each(0, chips * chunks, lambda i: tok_c(
        (i // chunks) * 2 + c, lax.rem(i, chunks)).wait_send())
    each(1, chips, lambda i: gain_copy(i).wait_send())
    each(0, chips, lambda i: gain_pair(i).wait_send())
    each(1, chips, lambda i: k_copy(i).wait_send())
    each(1, chips, lambda i: v_copy(i).wait_send())

    def core_sent(i):
        slot = i * 2 + c
        kv_pair(k_buf.at[slot], k_buf, k_send_c, k_recv, slot).wait_send()
        kv_pair(v_buf.at[slot], v_buf, v_send_c, v_recv, slot).wait_send()
        s1_copy(i).wait_send()

    each(0, chips, core_sent)
    for i in range(1, members):
        own_copy(0, k_own, i).wait_send()
        own_copy(1, v_own, i).wait_send()
    for d_y in range(1, ny):
        for k in range(cuts):
            each(0, nz, lambda d, d_y=d_y, k=k: s2_copy(d, d_y, k).wait_send())
    for k in range(cuts):
        each(1, nz, lambda d, k=k: s3_copy(d, k).wait_send())


def body(n, ny, tokens, gain, w_query, w_key, w_value, w_out, cache):
    rows, width = tokens.shape
    features = w_query.shape[1]
    heads = H // n
    chips = n // 2
    nz = chips // ny
    members = n // KV
    own = w_key.shape[0]
    positions = cache.shape[1]
    stack = heads * rows
    dma = pltpu.SemaphoreType.DMA
    hbm = pl.BlockSpec(memory_space=pl.ANY)
    vmem = pl.BlockSpec(memory_space=pltpu.VMEM)
    block = (rows, width)
    return pl.pallas_call(
        functools.partial(kernel, n, ny),
        out_shape=jax.ShapeDtypeStruct((rows, width), BF16),
        in_specs=[vmem, vmem, hbm, hbm, hbm, hbm, hbm],
        out_specs=vmem,
        scratch_shapes=[
            pltpu.VMEM((n, rows, width), BF16),
            pltpu.VMEM((1, width), F32),
            pltpu.VMEM((n, 1, width), F32),
            pltpu.VMEM((rows, features), BF16),
            pltpu.VMEM(w_query.shape, BF16),
            pltpu.VMEM(w_key.shape, BF16),
            pltpu.VMEM(w_value.shape, BF16),
            pltpu.VMEM(w_out.shape, BF16),
            pltpu.VMEM((rows, heads * DH), F32),
            pltpu.VMEM((own, rows), F32),
            pltpu.VMEM((own, rows), F32),
            pltpu.VMEM((stack, DH), BF16),
            pltpu.VMEM((members, own, rows), BF16),
            pltpu.VMEM((members, own, rows), BF16),
            pltpu.VMEM((n, positions, DH), BF16),
            pltpu.VMEM((n, positions, DH), BF16),
            pltpu.VMEM((n, stack, positions), F32),
            pltpu.VMEM((stack, 128), F32),
            pltpu.VMEM((stack, 128), F32),
            pltpu.VMEM((stack, DH), F32),
            pltpu.VMEM((rows, heads * DH), BF16),
            pltpu.VMEM((chips,) + block, F32),
            pltpu.VMEM((chips,) + block, BF16),
            pltpu.VMEM((chips,) + block, BF16),
            pltpu.VMEM((nz, ny) + block, BF16),
            pltpu.VMEM((nz, ny) + block, BF16),
            pltpu.VMEM((nz,) + block, BF16),
            pltpu.VMEM((nz,) + block, BF16),
            dma((8,)),
            dma((n,)), dma((n,)),
            dma((nz, CHUNKS)), dma((nz, CHUNKS)), dma((nz, ny, CHUNKS)), dma((chips, CHUNKS)),
            dma((n, CHUNKS)),
            dma((chips,)), dma((chips,)), dma((n,)),
            dma((chips,)), dma((chips,)), dma((n,)),
            dma((2, members)), dma((2, members)),
            dma((chips,)), dma((chips,)),
            dma((nz, ny, CUTS)), dma((nz, ny, CUTS)),
            dma((nz, CUTS)), dma((nz, CUTS)),
        ],
        compiler_params=pltpu.CompilerParams(
            collective_id=0, has_side_effects=True, vmem_limit_bytes=60 * 2**20
        ),
    )(tokens, gain, w_query, w_key, w_value, w_out, cache)


def solution(mesh):
    n = mesh.shape["seq"]
    ny = max(1, 4 // mesh.shape["group"])
    return jax.shard_map(
        functools.partial(body, n, ny),
        mesh=mesh,
        in_specs=(
            P("group", "seq"),
            P("seq"),
            P("seq", None),
            P("seq", None),
            P("seq", None),
            P("seq", None),
            P(None, ("group", "seq"), None),
        ),
        out_specs=P("group", "seq"),
        check_vma=False,
    )
```

```python
import functools
import math

import jax
import jax.numpy as jnp
from jax import lax
from jax.experimental import pallas as pl
from jax.experimental.pallas import tpu as pltpu
from jax.sharding import PartitionSpec as P

H = 64
KV = 8
DH = 128
CHUNKS = 2
CUTS = 2
NT = (((1,), (1,)), ((), ()))
MESH = pl.DeviceIdType.MESH
F32 = jnp.float32
BF16 = jnp.bfloat16


def kernel(
    n, ny, tokens, gain_in, w_query, w_key, w_value, w_out, cache, out,
    tok, my_gain, gains, normed, wq, wk, wv, wo, q_acc, k_acc, v_acc, q_rows, k_own, v_own,
    k_buf, v_buf, scores, top, low, numer, att, acc, s1_out, s1_in, s2_out, s2_in, s3_out, s3_in,
    local_sem, gain_send, gain_recv, tok_up, tok_down, tok_send_y, tok_send_c, tok_recv,
    k_send, k_send_c, k_recv, v_send, v_send_c, v_recv, own_send, own_recv,
    s1_send, s1_recv, s2_send, s2_recv, s3_send, s3_recv,
):
    chips = n // 2
    nz = chips // ny
    me = lax.axis_index("seq")
    c = lax.rem(me, 2)
    chip = me // 2
    y = lax.rem(chip, ny)
    z = chip // ny
    partner = chip * 2 + 1 - c
    rows, width = tokens.shape
    heads = H // n
    members = n // KV
    kv_head = me // members
    member = lax.rem(me, members)
    positions = cache.shape[1]
    lanes = [slice(k * 128, (k + 1) * 128) for k in range(positions // 128)]
    scale = 1.0 / math.sqrt(DH)

    def seq_of(z_, y_, c_):
        return (z_ * ny + y_) * 2 + c_

    def other_z(d):
        return lax.rem(z + d, nz)

    def other_y(d):
        return lax.rem(y + d, ny)

    def remote(src, dst, send, recv, to):
        return pltpu.make_async_remote_copy(
            src_ref=src, dst_ref=dst, send_sem=send, recv_sem=recv,
            device_id={"seq": to}, device_id_type=MESH,
        )

    def each(start, stop, step):
        lax.fori_loop(start, stop, lambda i, carry: (step(i), carry)[1], 0)

    weights_in = [
        pltpu.make_async_copy(src, dst, local_sem.at[i])
        for i, (src, dst) in enumerate(
            [(w_query, wq), (w_key, wk), (w_value, wv), (w_out, wo)]
        )
    ]
    own_tok = pltpu.make_async_copy(tokens, tok.at[me], local_sem.at[4])
    gain = my_gain

    def own_cols(to_kv):
        return pl.ds(pl.multiple_of(to_kv * DH, DH), DH)

    own_k = pltpu.make_async_copy(
        cache.at[0, :, own_cols(kv_head)], k_buf.at[me], local_sem.at[6]
    )
    own_v = pltpu.make_async_copy(
        cache.at[1, :, own_cols(kv_head)], v_buf.at[me], local_sem.at[7]
    )

    barrier = pltpu.get_barrier_semaphore()

    def greet(to):
        pl.semaphore_signal(barrier, inc=1, device_id={"seq": to}, device_id_type=MESH)

    @pl.when(z >= 1)
    def _():
        greet(seq_of(z - 1, y, c))

    @pl.when(z + 1 < nz)
    def _():
        greet(seq_of(z + 1, y, c))

    for d_y in range(1, ny):
        greet(seq_of(z, other_y(d_y), c))
    greet(partner)
    own_tok.start()
    for copy in weights_in:
        copy.start()
    my_gain[...] = gain_in[...].astype(F32).reshape(1, width)
    gains[me] = my_gain[...]
    pl.semaphore_wait(
        barrier, ny + jnp.where(z >= 1, 1, 0) + jnp.where(z + 1 < nz, 1, 0))

    chunks = tok_recv.shape[1]
    deep = rows // chunks

    def piece_of(slot, k):
        return tok.at[slot, pl.ds(pl.multiple_of(k * deep, deep), deep), :]

    def tok_z(slot, k, d, up):
        ends = tok_up if up else tok_down
        to = jnp.clip(z + (1 if up else -1), 0, nz - 1)
        return remote(piece_of(slot, k), piece_of(slot, k), ends.at[d, k],
                      tok_recv.at[slot, k], seq_of(to, y, c))

    def tok_y(slot, k, d_z, d_y):
        return remote(piece_of(slot, k), piece_of(slot, k), tok_send_y.at[d_z, d_y, k],
                      tok_recv.at[slot, k], seq_of(z, other_y(d_y), c))

    def tok_c(slot, k):
        return remote(piece_of(slot, k), piece_of(slot, k), tok_send_c.at[slot // 2, k],
                      tok_recv.at[slot, k], partner)

    def tok_wait(slot, k):
        remote(piece_of(slot, k), piece_of(slot, k), tok_send_c.at[0, k], tok_recv.at[slot, k],
               partner).wait_recv()

    own_tok.wait()

    def send_own(k):
        @pl.when(z + 1 < nz)
        def _():
            tok_z(me, k, 0, True).start()

        @pl.when(z >= 1)
        def _():
            tok_z(me, k, 0, False).start()

        for d_y in range(1, ny):
            tok_y(me, k, z, d_y).start()
        tok_c(me, k).start()

    each(0, chunks, send_own)

    def gain_copy(i):
        return remote(gain, gains.at[me], gain_send.at[i], gain_recv.at[me],
                      lax.rem(chip + i, chips) * 2 + c)

    def gain_pair(i):
        slot = lax.rem(chip + i, chips) * 2 + c
        return remote(gains.at[slot], gains.at[slot], gain_send.at[chips + i],
                      gain_recv.at[slot], partner)

    def kv_copy(half, buf, send, recv, i):
        other = lax.rem(chip + i, chips)
        to = other * 2 + c
        return remote(cache.at[half, :, own_cols(to // members)], buf.at[me], send.at[i],
                      recv.at[me], to)

    def kv_pair(src, buf, send, recv, slot):
        return remote(src, buf.at[slot], send.at[slot // 2], recv.at[slot], partner)

    def kv_wait(buf, send, recv, slot):
        remote(buf.at[slot], buf.at[slot], send.at[0], recv.at[slot], partner).wait_recv()

    def k_copy(i):
        return kv_copy(0, k_buf, k_send, k_recv, i)

    def v_copy(i):
        return kv_copy(1, v_buf, v_send, v_recv, i)


    def send_all(copy):
        for near, same in ((False, True), (False, False), (True, True), (True, False)):
            def go(i, near=near, same=same):
                other = lax.rem(chip + i, chips)
                in_row = lax.rem(other, ny) == y
                in_half = (other // ny < nz // 2) == (z < nz // 2)

                @pl.when((in_half if near else jnp.logical_not(in_half))
                         & (in_row if same else jnp.logical_not(in_row)))
                def _():
                    copy(i).start()

            each(1, chips, go)

    def forward_z(i):
        d = 1 + i // chunks
        k = lax.rem(i, chunks)

        def pass_on(slot, up):
            tok_wait(slot, k)

            @pl.when((z + 1 < nz) if up else (z >= 1))
            def _():
                tok_z(slot, k, d, up).start()

            for d_y in range(1, ny):
                tok_y(slot, k, slot // (2 * ny), d_y).start()
            tok_c(slot, k).start()

        @pl.when(z - d >= 0)
        def _():
            pass_on(seq_of(z - d, y, c), True)

        @pl.when(z + d < nz)
        def _():
            pass_on(seq_of(z + d, y, c), False)

    each(0, (nz - 1) * chunks, forward_z)
    each(1, chips, lambda i: gain_copy(i).start())
    gain_pair(0).start()
    send_all(k_copy)
    k_own_src = cache.at[0, :, own_cols(kv_head)]
    v_own_src = cache.at[1, :, own_cols(kv_head)]
    kv_pair(k_own_src, k_buf, k_send_c, k_recv, me).start()
    own_k.start()


    def spread(i):
        reach = jnp.minimum(z, nz - 1 - z)
        side = jnp.where(lax.rem(i, 2) == 1, z - (i + 1) // 2, z + i // 2)
        return jnp.where(i <= 2 * reach, side, jnp.where(z < nz - 1 - z, i, nz - 1 - i))

    for d_y in range(1, ny):
        def forward_y(i, d_y=d_y):
            there = seq_of(spread(i // chunks), other_y(d_y), c)
            k = lax.rem(i, chunks)
            tok_wait(there, k)
            tok_c(there, k).start()
        each(0, nz * chunks, forward_y)

    send_all(v_copy)

    def gain_wait(slot):
        remote(gain, gains.at[slot], gain_send.at[0], gain_recv.at[slot], partner).wait_recv()

    def gain_step(i):
        gain_wait(lax.rem(chip + i, chips) * 2 + c)
        gain_pair(i).start()

    each(1, chips, gain_step)
    kv_pair(v_own_src, v_buf, v_send_c, v_recv, me).start()
    own_v.start()

    each(0, chips * chunks, lambda i: tok_wait((i // chunks) * 2 + 1 - c, lax.rem(i, chunks)))

    parts = width // 128

    def square_step(b, total):
        x = tok[b].astype(F32)
        for k in range(parts):
            piece = x[:, k * 128:(k + 1) * 128]
            total = total + piece * piece
        return total

    total = lax.fori_loop(0, n, square_step, jnp.zeros((rows, 128), F32))
    each(0, chips, lambda i: gain_wait(i * 2 + 1 - c))
    mean = jnp.sum(total, axis=1, keepdims=True) * (1.0 / (n * width))
    inverse = jnp.broadcast_to(lax.rsqrt(mean + 1e-05), (rows, 128))

    def norm_step(b):
        for k in range(parts):
            x = tok[b, :, k * 128:(k + 1) * 128].astype(F32)
            g = gains[b, :, k * 128:(k + 1) * 128].astype(F32)
            normed[:, pl.ds(pl.multiple_of(b * width + k * 128, 128), 128)] = (
                x * inverse * g).astype(BF16)

    each(0, n, norm_step)

    for copy in weights_in[:3]:
        copy.wait()
    q_acc[...] = jnp.zeros_like(q_acc)
    k_acc[...] = jnp.zeros_like(k_acc)
    v_acc[...] = jnp.zeros_like(v_acc)
    depth = 1024

    def project(i):
        cols = pl.ds(pl.multiple_of(i * depth, depth), depth)
        x = normed[:, cols]
        k_acc[...] += lax.dot_general(wk[:, cols], x, NT, preferred_element_type=F32)
        v_acc[...] += lax.dot_general(wv[:, cols], x, NT, preferred_element_type=F32)
        q_acc[...] += lax.dot_general(x, wq[:, cols], NT, preferred_element_type=F32)

    each(0, normed.shape[1] // depth, project)
    k_own[member] = k_acc[...].astype(BF16)
    v_own[member] = v_acc[...].astype(BF16)

    def own_copy(which, buf, i):
        return remote(buf.at[member], buf.at[member], own_send.at[which, i],
                      own_recv.at[which, member], kv_head * members + lax.rem(member + i, members))

    def own_wait(which, buf, i):
        slot = lax.rem(member + i, members)
        remote(buf.at[slot], buf.at[slot], own_send.at[which, 0], own_recv.at[which, slot],
               partner).wait_recv()

    for i in range(1, members):
        own_copy(0, k_own, i).start()
        own_copy(1, v_own, i).start()

    for h in range(heads):
        q_rows[h * rows:(h + 1) * rows, :] = q_acc[:, h * DH:(h + 1) * DH].astype(BF16)

    top[...] = jnp.full_like(top, -jnp.inf)

    def score_block(slot):
        keys = k_buf[slot]
        for h in range(heads):
            here = slice(h * rows, (h + 1) * rows)
            s = lax.dot_general(q_rows[here, :], keys, NT, preferred_element_type=F32) * scale
            scores[slot, here, :] = s
            best = top[here, :]
            for part in lanes:
                best = jnp.maximum(best, s[:, part])
            top[here, :] = best

    own_k.wait()
    score_block(me)

    def k_mine(i):
        slot = lax.rem(chip + chips - i, chips) * 2 + c
        kv_wait(k_buf, k_send_c, k_recv, slot)
        kv_pair(k_buf.at[slot], k_buf, k_send_c, k_recv, slot).start()
        score_block(slot)

    each(1, chips, k_mine)

    def k_theirs(i):
        slot = lax.rem(chip + chips - i, chips) * 2 + 1 - c
        kv_wait(k_buf, k_send_c, k_recv, slot)
        score_block(slot)

    each(0, chips, k_theirs)

    for i in range(1, members):
        own_wait(0, k_own, i)
        own_wait(1, v_own, i)
    key_rows = k_own[...].astype(F32).reshape(DH, rows).T
    own_scores = []
    for h in range(heads):
        here = slice(h * rows, (h + 1) * rows)
        own = jnp.sum(q_rows[here, :].astype(F32) * key_rows, axis=1, keepdims=True) * scale
        best = jnp.maximum(jnp.max(top[here, :], axis=1, keepdims=True), own)
        top[here, :] = jnp.broadcast_to(best, (rows, 128))
        own_scores.append(jnp.exp(own - best))

    low[...] = jnp.zeros_like(low)
    numer[...] = jnp.zeros_like(numer)

    def value_block(slot):
        values = v_buf[slot]
        for h in range(heads):
            here = slice(h * rows, (h + 1) * rows)
            best = top[here, :]
            pieces = [jnp.exp(scores[slot, here, part] - best) for part in lanes]
            low[here, :] += functools.reduce(jnp.add, pieces)
            weights = jnp.concatenate([piece.astype(BF16) for piece in pieces], axis=1)
            numer[here, :] += jnp.dot(weights, values, preferred_element_type=F32)

    own_v.wait()
    value_block(me)

    def v_mine(i):
        slot = lax.rem(chip + chips - i, chips) * 2 + c
        kv_wait(v_buf, v_send_c, v_recv, slot)
        kv_pair(v_buf.at[slot], v_buf, v_send_c, v_recv, slot).start()
        value_block(slot)

    each(1, chips, v_mine)

    def v_theirs(i):
        slot = lax.rem(chip + chips - i, chips) * 2 + 1 - c
        kv_wait(v_buf, v_send_c, v_recv, slot)
        value_block(slot)

    each(0, chips, v_theirs)

    value_rows = v_own[...].astype(F32).reshape(DH, rows).T
    for h in range(heads):
        here = slice(h * rows, (h + 1) * rows)
        own_weight = own_scores[h]
        denom = jnp.sum(low[here, :], axis=1, keepdims=True) + own_weight
        total = numer[here, :] + own_weight.astype(BF16).astype(F32) * value_rows
        att[:, h * DH:(h + 1) * DH] = (total / denom).astype(BF16)

    weights_in[3].wait()

    def partial_for(to):
        cols = pl.ds(pl.multiple_of(to * width, width), width)
        return jnp.dot(att[...], wo[:, cols], preferred_element_type=F32)

    def s1_copy(target):
        return remote(s1_out.at[target], s1_in.at[target], s1_send.at[target],
                      s1_recv.at[target], partner)

    cuts = s2_send.shape[2]
    short = rows // cuts
    pieces = [slice(k * short, (k + 1) * short) for k in range(cuts)]

    def s2_copy(d_z, d_y, k):
        return remote(s2_out.at[d_z, d_y, pieces[k]], s2_in.at[d_z, d_y, pieces[k]],
                      s2_send.at[d_z, d_y, k], s2_recv.at[d_z, d_y, k], seq_of(z, other_y(d_y), c))

    def s3_copy(d, k):
        return remote(s3_out.at[d, pieces[k]], s3_in.at[d, pieces[k]], s3_send.at[d, k],
                      s3_recv.at[d, k], seq_of(other_z(d), y, c))

    def distance(i):
        down = nz - 1 - i
        down = jnp.where(down <= z, down - 1, down)
        up = jnp.where(i >= z, i + 1, i)
        there = jnp.where(z < nz - 1 - z, down, up)
        return lax.rem(jnp.where(i == nz - 1, z, there) - z + nz, nz)

    def give(i, d_y):
        target = other_z(distance(i)) * ny + other_y(d_y)
        s1_out[target] = partial_for(target * 2 + 1 - c).astype(BF16)
        s1_copy(target).start()

    def keep(i, d_y):
        target = other_z(distance(i)) * ny + other_y(d_y)
        acc[target] = partial_for(target * 2 + c)

    def step_two(i, d_y):
        d = distance(i)
        keep(i, d_y)
        target = other_z(d) * ny + other_y(d_y)
        s1_copy(target).wait_recv()
        for k, here in enumerate(pieces):
            s2_out[d, d_y, here, :] = (
                acc[target, here, :] + s1_in[target, here, :].astype(F32)).astype(BF16)
            s2_copy(d, d_y, k).start()

    def column_sum(d, k):
        here = pieces[k]
        target = other_z(d) * ny + y
        total = acc[target, here, :] + s1_in[target, here, :].astype(F32)
        for d_y in range(1, ny):
            s2_copy(d, d_y, k).wait_recv()
            total = total + s2_in[d, d_y, here, :].astype(F32)
        return total

    def step_three(i):
        d = distance(i)
        s1_copy(other_z(d) * ny + y).wait_recv()
        for k, here in enumerate(pieces):
            s3_out[d, here, :] = column_sum(d, k).astype(BF16)
            s3_copy(d, k).start()

    for d_y in range(1, ny):
        each(0, nz, functools.partial(give, d_y=d_y))
        each(0, nz, functools.partial(step_two, d_y=d_y))
    each(0, nz, functools.partial(give, d_y=0))
    each(0, nz, functools.partial(keep, d_y=0))
    each(0, nz - 1, step_three)
    s1_copy(chip).wait_recv()
    for k, here in enumerate(pieces):
        acc[chip, here, :] = column_sum(0, k)

    def last(d):
        for k, here in enumerate(pieces):
            s3_copy(d, k).wait_recv()
            acc[chip, here, :] += s3_in[d, here, :].astype(F32)

    each(1, nz, last)
    out[...] = acc[chip].astype(out.dtype)

    def tok_sent(i):
        d = i // chunks
        k = lax.rem(i, chunks)

        @pl.when((z - d >= 0) & (z + 1 < nz))
        def _():
            tok_z(seq_of(z - d, y, c), k, d, True).wait_send()

        @pl.when((z + d < nz) & (z >= 1))
        def _():
            tok_z(seq_of(z + d, y, c), k, d, False).wait_send()

        for d_y in range(1, ny):
            tok_y(me, k, d, d_y).wait_send()

    each(0, nz * chunks, tok_sent)
    each(0, chips * chunks, lambda i: tok_c(
        (i // chunks) * 2 + c, lax.rem(i, chunks)).wait_send())
    each(1, chips, lambda i: gain_copy(i).wait_send())
    each(0, chips, lambda i: gain_pair(i).wait_send())
    each(1, chips, lambda i: k_copy(i).wait_send())
    each(1, chips, lambda i: v_copy(i).wait_send())

    def core_sent(i):
        slot = i * 2 + c
        kv_pair(k_buf.at[slot], k_buf, k_send_c, k_recv, slot).wait_send()
        kv_pair(v_buf.at[slot], v_buf, v_send_c, v_recv, slot).wait_send()
        s1_copy(i).wait_send()

    each(0, chips, core_sent)
    for i in range(1, members):
        own_copy(0, k_own, i).wait_send()
        own_copy(1, v_own, i).wait_send()
    for d_y in range(1, ny):
        for k in range(cuts):
            each(0, nz, lambda d, d_y=d_y, k=k: s2_copy(d, d_y, k).wait_send())
    for k in range(cuts):
        each(1, nz, lambda d, k=k: s3_copy(d, k).wait_send())


def body(n, ny, tokens, gain, w_query, w_key, w_value, w_out, cache):
    rows, width = tokens.shape
    features = w_query.shape[1]
    heads = H // n
    chips = n // 2
    nz = chips // ny
    members = n // KV
    own = w_key.shape[0]
    positions = cache.shape[1]
    stack = heads * rows
    dma = pltpu.SemaphoreType.DMA
    hbm = pl.BlockSpec(memory_space=pl.ANY)
    vmem = pl.BlockSpec(memory_space=pltpu.VMEM)
    block = (rows, width)
    return pl.pallas_call(
        functools.partial(kernel, n, ny),
        out_shape=jax.ShapeDtypeStruct((rows, width), BF16),
        in_specs=[vmem, vmem, hbm, hbm, hbm, hbm, hbm],
        out_specs=vmem,
        scratch_shapes=[
            pltpu.VMEM((n, rows, width), BF16),
            pltpu.VMEM((1, width), F32),
            pltpu.VMEM((n, 1, width), F32),
            pltpu.VMEM((rows, features), BF16),
            pltpu.VMEM(w_query.shape, BF16),
            pltpu.VMEM(w_key.shape, BF16),
            pltpu.VMEM(w_value.shape, BF16),
            pltpu.VMEM(w_out.shape, BF16),
            pltpu.VMEM((rows, heads * DH), F32),
            pltpu.VMEM((own, rows), F32),
            pltpu.VMEM((own, rows), F32),
            pltpu.VMEM((stack, DH), BF16),
            pltpu.VMEM((members, own, rows), BF16),
            pltpu.VMEM((members, own, rows), BF16),
            pltpu.VMEM((n, positions, DH), BF16),
            pltpu.VMEM((n, positions, DH), BF16),
            pltpu.VMEM((n, stack, positions), F32),
            pltpu.VMEM((stack, 128), F32),
            pltpu.VMEM((stack, 128), F32),
            pltpu.VMEM((stack, DH), F32),
            pltpu.VMEM((rows, heads * DH), BF16),
            pltpu.VMEM((chips,) + block, F32),
            pltpu.VMEM((chips,) + block, BF16),
            pltpu.VMEM((chips,) + block, BF16),
            pltpu.VMEM((nz, ny) + block, BF16),
            pltpu.VMEM((nz, ny) + block, BF16),
            pltpu.VMEM((nz,) + block, BF16),
            pltpu.VMEM((nz,) + block, BF16),
            dma((8,)),
            dma((n,)), dma((n,)),
            dma((nz, CHUNKS)), dma((nz, CHUNKS)), dma((nz, ny, CHUNKS)), dma((chips, CHUNKS)),
            dma((n, CHUNKS)),
            dma((chips,)), dma((chips,)), dma((n,)),
            dma((chips,)), dma((chips,)), dma((n,)),
            dma((2, members)), dma((2, members)),
            dma((chips,)), dma((chips,)),
            dma((nz, ny, CUTS)), dma((nz, ny, CUTS)),
            dma((nz, CUTS)), dma((nz, CUTS)),
        ],
        compiler_params=pltpu.CompilerParams(
            collective_id=0, has_side_effects=True, vmem_limit_bytes=60 * 2**20
        ),
    )(tokens, gain, w_query, w_key, w_value, w_out, cache)


def solution(mesh):
    n = mesh.shape["seq"]
    ny = max(1, 4 // mesh.shape["group"])
    return jax.shard_map(
        functools.partial(body, n, ny),
        mesh=mesh,
        in_specs=(
            P("group", "seq"),
            P("seq"),
            P("seq", None),
            P("seq", None),
            P("seq", None),
            P("seq", None),
            P(None, ("group", "seq"), None),
        ),
        out_specs=P("group", "seq"),
        check_vma=False,
    )
```
